512 devices in a mesh: shot: 16 (over x, z_lo), tx: 8 (over z_hi, core), ty: 4 (over y).
Axes of the slice: x: 4, y: 4, z: 16 (z_hi: 4, z_lo: 4; z = z_hi * 4 + z_lo), core: 2. Of those that a mesh axis runs over, the one named last changes fastest.
Arguments:
- adjoint_prior: float32 [16, 32, 256, 512], P('shot', None, 'tx', 'ty'), may hold values from -6 to 6
- adjoint_now: float32 [16, 32, 256, 512], P('shot', None, 'tx', 'ty'), may hold values from -6 to 6
- forward_saved: float32 [16, 2, 32, 256, 512], P('shot', None, None, 'tx', 'ty'), may hold values from -6 to 6
- residuals: float32 [16, 10, 1024], P('shot'), may hold values from -6 to 6
- receiver_x: int32 [16, 1024], P('shot'), may hold values from 0 to 255
- receiver_y: int32 [16, 1024], P('shot'), may hold values from 0 to 511
- source_x: int32 [16], P('shot'), may hold values from 0 to 255
- source_y: int32 [16], P('shot'), may hold values from 0 to 511
- saved_slot: int32 [10], replicated, may hold values from 0 to 1
- model: float32 [32, 256, 512], P('shot', 'tx', 'ty'), may hold values from 0.03 to 0.12
Outputs:
- adjoint_state: float32 [16, 32, 256, 512], P('shot', None, 'tx', 'ty')
- gradient: float32 [32, 256, 512], P('shot', 'tx', 'ty')
- updated_model: float32 [32, 256, 512], P('shot', 'tx', 'ty')
The draws below stay inside these ranges and needn't reach their ends.
All inputs are finite; a program needn't handle non-finite values.
Results may differ from the reference program's by a relative error of at most 0.0001.
Values sent between devices are 32-bit elements; how exact they have to be, the bound alone decides.
A program may use at most 64 MiB of HBM per device.

```python
import math
import jax
import jax.numpy as jnp
from jax import lax

NZ = 32
STEPS = 10
SAVED = 2
NREC = 1024
SHOTS = 16
NX = 256
NY = 512


def with_ends(values, rng, low, largest):
    extent = values.shape
    index_at = [jax.random.randint(jax.random.fold_in(rng, axis), (), 0, extent[axis]) for axis in range(len(extent))]
    values = values.at[tuple(index_at)].set(low)
    longest = extent.index(max(extent))
    index_at[longest] = (index_at[longest] + 1) % extent[longest]
    return values.at[tuple(index_at)].set(largest)


def steps_of(rng, extent, cuts, low, top_value):
    loudness = 1.0
    for dim, parts in cuts:
        heights = jax.random.uniform(jax.random.fold_in(jax.random.fold_in(rng, 6), dim), (parts,), jnp.float32, low / len(cuts), top_value / len(cuts))
        loudness = loudness * jnp.repeat(jnp.exp(heights), extent[dim] // parts).reshape((-1,) + (1,) * (len(extent) - 1 - dim))
    return loudness


def centred(key, dims, spread, limit, split=(), kind=jnp.bfloat16):
    result = spread * jax.random.normal(key, dims, jnp.float32)
    if split:
        result = result * steps_of(key, dims, split, -0.22, 0.18)
    return jnp.clip(result, -limit, limit).astype(kind)


def setup_inputs(seed: int = 0) -> dict:
    streams_of = jax.random.split(jax.random.key(seed), 11)
    return {
        "adjoint_prior": centred(streams_of[0], (SHOTS, NZ, NX, NY), 1.0, 6.0, ((0, 16), (2, 8), (3, 4)), jnp.float32),
        "adjoint_now": centred(streams_of[1], (SHOTS, NZ, NX, NY), 1.0, 6.0, ((0, 16), (2, 8), (3, 4)), jnp.float32),
        "forward_saved": centred(streams_of[2], (SHOTS, SAVED, NZ, NX, NY), 1.0, 6.0, ((0, 16), (3, 8), (4, 4)), jnp.float32),
        "residuals": centred(streams_of[3], (SHOTS, STEPS, NREC), 1.0, 6.0, ((0, 16),), jnp.float32),
        "receiver_x": with_ends(jax.random.randint(streams_of[4], (SHOTS, NREC), 0, NX), jax.random.fold_in(streams_of[4], 1), 0, NX - 1).astype(jnp.int32),
        "receiver_y": with_ends(jax.random.randint(streams_of[5], (SHOTS, NREC), 0, NY), jax.random.fold_in(streams_of[5], 1), 0, NY - 1).astype(jnp.int32),
        "source_x": with_ends(jax.random.randint(streams_of[6], (SHOTS,), 0, NX), jax.random.fold_in(streams_of[6], 1), 0, NX - 1).astype(jnp.int32),
        "source_y": with_ends(jax.random.randint(streams_of[7], (SHOTS,), 0, NY), jax.random.fold_in(streams_of[7], 1), 0, NY - 1).astype(jnp.int32),
        "saved_slot": with_ends(jax.random.randint(streams_of[8], (STEPS,), 0, SAVED), jax.random.fold_in(streams_of[8], 1), 0, SAVED - 1).astype(jnp.int32),
        "model": jnp.clip(0.03 + 0.089999998 * jax.random.uniform(streams_of[9], (NZ, NX, NY), jnp.float32) ** steps_of(streams_of[9], (NZ, NX, NY), ((0, 16), (1, 8), (2, 4)), -0.2, 0.2), 0.03, 0.12),
    }


rec_depth = 2
src_depth = 3.0
mute_radius = 10.0
step_size = 0.01

def coefficients():
    weights_table = []
    for offset in range(1, 9):
        weights_table.append(2.0 * (-1.0) ** (offset + 1) * math.factorial(8) ** 2 / (offset * offset * math.factorial(8 - offset) * math.factorial(8 + offset)))
    centre = -2.0 * sum(weights_table)
    return (centre, weights_table)

def laplace(padded):
    centre, weights_table = coefficients()
    span_x = padded.shape[-2] - 16
    span_y = padded.shape[-1] - 16
    depth_cells = padded.shape[-3]
    interior = padded[..., 8:8 + span_x, 8:8 + span_y]
    pad_spec = [(0, 0)] * (padded.ndim - 3) + [(8, 8), (0, 0), (0, 0)]
    column = jnp.pad(interior, pad_spec)
    summed = 3.0 * centre * interior
    for offset in range(1, 9):
        weight = weights_table[offset - 1]
        neighbours = padded[..., 8 + offset:8 + offset + span_x, 8:8 + span_y] + padded[..., 8 - offset:8 - offset + span_x, 8:8 + span_y]
        neighbours = neighbours + padded[..., 8:8 + span_x, 8 + offset:8 + offset + span_y] + padded[..., 8:8 + span_x, 8 - offset:8 - offset + span_y]
        neighbours = neighbours + column[..., 8 + offset:8 + offset + depth_cells, :, :] + column[..., 8 - offset:8 - offset + depth_cells, :, :]
        summed = summed + weight * neighbours
    return summed

def reference(adjoint_prior, adjoint_now, forward_saved, residuals, receiver_x, receiver_y, source_x, source_y, saved_slot, model):
    cells_z = jnp.arange(NZ, dtype=jnp.float32) - src_depth
    cells_x = jnp.arange(NX, dtype=jnp.int32).astype(jnp.float32)
    cells_y = jnp.arange(NY, dtype=jnp.int32).astype(jnp.float32)

    def one_shot(packed):
        previous, current, saved, traces, rec_x, rec_y, src_x, src_y = packed
        imaging = jnp.zeros((NZ, NX, NY), jnp.float32)
        for offset in range(STEPS):
            moment = STEPS - 1 - offset
            padded = jnp.pad(current, ((0, 0), (8, 8), (8, 8)))
            updated = 2.0 * current - previous + model * laplace(padded)
            surface = jnp.zeros((NX, NY), jnp.float32).at[rec_x, rec_y].add(traces[moment])
            updated = updated.at[rec_depth].add(surface)
            snapshot = lax.dynamic_index_in_dim(saved, saved_slot[moment].astype(jnp.int32), 0, keepdims=False)
            imaging = imaging + snapshot * updated
            previous, current = (current, updated)
        gap_x = cells_x - src_x.astype(jnp.float32)
        gap_y = cells_y - src_y.astype(jnp.float32)
        distance = (cells_z * cells_z)[:, None, None] + (gap_x * gap_x)[None, :, None] + (gap_y * gap_y)[None, None, :]
        mute_factor = 1.0 - jnp.exp(-distance / (mute_radius * mute_radius))
        return (current, mute_factor * imaging)
    finals, muted = lax.map(one_shot, (adjoint_prior, adjoint_now, forward_saved, residuals, receiver_x, receiver_y, source_x, source_y))
    grad_scale = 1.0 / math.sqrt(SHOTS * STEPS)
    gradient = lax.optimization_barrier(jnp.sum(muted, axis=0)) * grad_scale
    updated_model = model - step_size * gradient
    return (finals, gradient, updated_model)
```

```python
import math

import jax
import jax.numpy as jnp
from jax import lax
from jax.experimental import pallas as pl
from jax.experimental.pallas import tpu as pltpu
from jax.sharding import PartitionSpec as P

STEPS = 10
REACH = 8
SPLIT = 4

rec_depth = 2
src_depth = 3.0
mute_radius = 10.0
step_size = 0.01

MESH = pl.DeviceIdType.MESH
F32 = jnp.float32
BF16 = jnp.bfloat16


def coefficients():
    weights_table = []
    for offset in range(1, 9):
        weights_table.append(
            2.0
            * (-1.0) ** (offset + 1)
            * math.factorial(8) ** 2
            / (offset * offset * math.factorial(8 - offset) * math.factorial(8 + offset))
        )
    centre = -2.0 * sum(weights_table)
    return (centre, weights_table)


def halves(value):
    high = value.astype(BF16)
    low = (value - high.astype(F32)).astype(BF16)
    return high, low


def kernel(
    prior_ref,
    now_ref,
    fwd_ref,
    res_ref,
    rx_ref,
    ry_ref,
    sx_ref,
    sy_ref,
    slot_ref,
    model_ref,
    out_ref,
    grad_ref,
    upd_ref,
    field,
    speed,
    saved,
    image,
    surface,
    ylap,
    band,
    xin,
    yout,
    yin,
    pass_in,
    pass_out,
    near_in,
    part,
    last_in,
    load_sem,
    x_send,
    x_recv,
    y_send,
    y_recv,
    gz_send,
    gz_recv,
    gx_send,
    gx_recv,
    gr_send,
    gr_recv,
    ra_send,
    ra_recv,
    rb_send,
    rb_recv,
    rd_send,
    rd_recv,
):
    centre, weights = coefficients()
    depth, span_x, span_y = speed.shape
    layers = depth // SPLIT
    tiles = span_x // 8
    shot, tx, ty = lax.axis_index("shot"), lax.axis_index("tx"), lax.axis_index("ty")
    zl, col = lax.rem(shot, 4), lax.div(shot, 4)
    right, left = lax.rem(col + 1, 4), lax.rem(col + 3, 4)
    opposite = lax.rem(col + 2, 4)
    to_right = {"shot": right * 4 + zl}
    to_left = {"shot": left * 4 + zl}
    x_ends = ((tx > 0, {"tx": tx - 1}), (tx < lax.axis_size("tx") - 1, {"tx": tx + 1}))
    y_ends = ((ty > 0, {"ty": ty - 1}), (ty < lax.axis_size("ty") - 1, {"ty": ty + 1}))

    def zl_peer(distance):
        return lax.rem(zl + distance, 4)

    loads = [
        pltpu.make_async_copy(
            now_ref.at[0], field.at[0, pl.ds(8, depth), pl.ds(8, span_x), :], load_sem.at[0]
        ),
        pltpu.make_async_copy(
            prior_ref.at[0], field.at[1, pl.ds(8, depth), pl.ds(8, span_x), :], load_sem.at[1]
        ),
        pltpu.make_async_copy(fwd_ref.at[0], saved, load_sem.at[2]),
        pltpu.make_async_copy(model_ref, speed.at[pl.ds(2 * shot, 2)], load_sem.at[3]),
    ]
    for load in loads:
        load.start()

    xin[...] = jnp.zeros_like(xin)
    yin[...] = jnp.zeros_like(yin)

    barrier = pltpu.get_barrier_semaphore()
    for present, peer in x_ends + y_ends:

        @pl.when(present)
        def _(peer=peer):
            pl.semaphore_signal(barrier, inc=1, device_id=peer, device_id_type=MESH)

    for distance in (1, 2, 3):
        pl.semaphore_signal(
            barrier, inc=1, device_id={"shot": col * 4 + zl_peer(distance)}, device_id_type=MESH
        )
    for peer in (to_right, to_left):
        pl.semaphore_signal(barrier, inc=1, device_id=peer, device_id_type=MESH)
    for par in range(2):
        field[par, pl.ds(0, 8)] = jnp.zeros((8, span_x + 16, span_y), F32)
        field[par, pl.ds(depth + 8, 8)] = jnp.zeros((8, span_x + 16, span_y), F32)
        field[par, pl.ds(8, depth), pl.ds(0, 8)] = jnp.zeros((depth, 8, span_y), F32)
        field[par, pl.ds(8, depth), pl.ds(span_x + 8, 8)] = jnp.zeros((depth, 8, span_y), F32)
    neighbours = 5
    for present, _ in x_ends + y_ends:
        neighbours = neighbours + present.astype(jnp.int32)
    pl.semaphore_wait(barrier, neighbours)

    def gather_z(distance):
        return pltpu.make_async_remote_copy(
            src_ref=model_ref,
            dst_ref=speed.at[pl.ds(2 * shot, 2)],
            send_sem=gz_send.at[distance - 1],
            recv_sem=gz_recv.at[distance - 1],
            device_id={"shot": col * 4 + zl_peer(distance)},
            device_id_type=MESH,
        )

    def gather_x(block, side):
        where = pl.ds(2 * (col * 4 + zl_peer(4 - block)), 2)
        return pltpu.make_async_remote_copy(
            src_ref=model_ref if block == 0 else speed.at[where],
            dst_ref=speed.at[where],
            send_sem=gx_send.at[block, side],
            recv_sem=gx_recv.at[block, side],
            device_id=to_right if side else to_left,
            device_id_type=MESH,
        )

    def gather_relay(block):
        origin = left if block < 2 else right
        where = pl.ds(2 * (origin * 4 + zl_peer(4 - block)), 2)
        return pltpu.make_async_remote_copy(
            src_ref=speed.at[where],
            dst_ref=speed.at[where],
            send_sem=gr_send.at[block],
            recv_sem=gr_recv.at[block],
            device_id=to_right if block < 2 else to_left,
            device_id_type=MESH,
        )

    def x_copy(par, c, side, source):
        zs = pl.ds(layers * c, layers)
        if source is None:
            src = field.at[par, pl.ds(8 + layers * c, layers), pl.ds(8 + (span_x - 8) * side, 8), :]
        else:
            src = source.at[0, zs, pl.ds((span_x - 8) * side, 8), :]
        return pltpu.make_async_remote_copy(
            src_ref=src,
            dst_ref=xin.at[par, c, 1 - side, :, pl.ds(8 * (1 - side), 8), :],
            send_sem=x_send.at[par, c, side],
            recv_sem=x_recv.at[par, c, 1 - side],
            device_id=x_ends[side][1],
            device_id_type=MESH,
        )

    def y_copy(par, c, side):
        return pltpu.make_async_remote_copy(
            src_ref=yout.at[par, c],
            dst_ref=yin.at[par, c, 1 - side],
            send_sem=y_send.at[par, c, side],
            recv_sem=y_recv.at[par, c, 1 - side],
            device_id=y_ends[side][1],
            device_id_type=MESH,
        )

    def each_end(ends, action):
        for side in range(2):

            @pl.when(ends[side][0])
            def _(side=side):
                action(side)

    for distance in (1, 2, 3):
        gather_z(distance).start()
    for side in range(2):
        gather_x(0, side).start()
    for c in range(SPLIT):
        each_end(x_ends, lambda side, c=c: x_copy(0, c, side, now_ref).start())

    lane = lax.broadcasted_iota(jnp.int32, (8, span_y), 1)
    group = lax.div(lane, 16)
    from_left = lax.rem(lane, 16) < 8

    def pack_y(par, c):
        for t in range(tiles):
            packed = jnp.zeros((8, span_y), F32)
            for j in range(layers):
                value = field[par, 8 + layers * c + j, pl.ds(8 + 8 * t, 8), :]
                packed = jnp.where(group == j, pltpu.roll(value, (16 * j + 8) % span_y, 1), packed)
            yout[par, c, t] = packed

    loads[0].wait()
    for c in range(SPLIT):
        pack_y(0, c)
        each_end(y_ends, lambda side, c=c: y_copy(0, c, side).start())

    row = lax.broadcasted_iota(jnp.int32, (span_y, span_y), 0)
    column = lax.broadcasted_iota(jnp.int32, (span_y, span_y), 1)
    away = jnp.abs(row - column)
    inner = lax.rem(row, 16)
    halo_away = jnp.where(inner < 8, column + 8 - inner, span_y - 8 + inner - column)
    own = jnp.zeros((span_y, span_y), F32)
    edge = jnp.zeros((span_y, span_y), F32)
    for k in range(1, 9):
        own = jnp.where(away == k, F32(weights[k - 1]), own)
        edge = jnp.where(halo_away == k, F32(weights[k - 1]), edge)
    for i, matrix in enumerate((own, edge)):
        high, low = halves(matrix)
        band[pl.ds(256 * i, 128), pl.ds(0, 128)] = high
        band[pl.ds(256 * i, 128), pl.ds(128, 128)] = low
        band[pl.ds(256 * i + 128, 128), pl.ds(0, 128)] = high
        band[pl.ds(256 * i + 128, 128), pl.ds(128, 128)] = jnp.zeros((128, 128), BF16)

    for block in (1, 2, 3):
        gather_z(block).wait_recv()
        for side in range(2):
            gather_x(block, side).start()

    count = rx_ref.shape[1]
    local_x = rx_ref[...] - tx * span_x
    local_y = ry_ref[...] - ty * span_y
    at_x = local_x == lax.broadcasted_iota(jnp.int32, (span_x, count), 0)
    at_y = (local_y == lax.broadcasted_iota(jnp.int32, (span_y, count), 0)).astype(F32).astype(BF16)

    def spread(moment, carry):
        traces = jnp.where(at_x, res_ref[0, pl.ds(moment, 1), :], 0.0)
        high = traces.astype(BF16)
        rest = traces - high.astype(F32)
        mid = rest.astype(BF16)
        low = (rest - mid.astype(F32)).astype(BF16)
        total = jnp.zeros((span_x, span_y), F32)
        for term in (low, mid, high):
            total = total + lax.dot_general(
                term, at_y, (((1,), (1,)), ((), ())), preferred_element_type=F32
            )
        surface[moment] = total
        return carry

    lax.fori_loop(0, STEPS, spread, 0)

    for block in range(4):
        gather_x(block, 1).wait_recv()
        if block < 2:
            gather_relay(block).start()
        gather_x(block, 0).wait_recv()
        if block >= 2:
            gather_relay(block).start()
    for block in range(4):
        gather_relay(block).wait_recv()
    for load in loads[1:]:
        load.wait()

    def zero_image(z, carry):
        image[z] = jnp.zeros((span_x, span_y), F32)
        return carry

    lax.fori_loop(0, depth, zero_image, 0)

    def before(n, c):
        par = lax.rem(n, 2)

        @pl.when(n > 0)
        def _():
            each_end(x_ends, lambda side: x_copy(1 - par, c, side, None).wait_send())
            each_end(y_ends, lambda side: y_copy(1 - par, c, side).wait_send())

        each_end(y_ends, lambda side: y_copy(par, c, 1 - side).wait_recv())
        base = layers * c
        value = field[par, pl.ds(8 + base, layers), pl.ds(8, span_x), :].reshape(
            layers * span_x, span_y
        )
        high, low = halves(value)
        halo = []
        for t in range(tiles):
            halo.append(jnp.where(from_left, yin[par, c, 0, t], yin[par, c, 1, t]))
        halo = jnp.concatenate(halo, axis=0)
        groups = lax.div(lax.broadcasted_iota(jnp.int32, (span_x, span_y), 1), 16)
        halo = jnp.concatenate([jnp.where(groups == j, halo, 0.0) for j in range(layers)], axis=0)
        halo_high, halo_low = halves(halo)
        sides = jnp.dot(
            jnp.concatenate([high, low, halo_high, halo_low], axis=1),
            band[...],
            preferred_element_type=F32,
        )
        ylap[...] = (sides[:, :span_y] + sides[:, span_y:]).reshape(layers, span_x, span_y)
        for t in range(tiles):
            rows = pl.ds(8 + 8 * t, 8)
            plane = [field[par, base + i, rows, :] for i in range(layers + 16)]
            for j in range(layers):
                total = ylap[j, pl.ds(8 * t, 8), :]
                for k in range(1, 9):
                    pairs = (plane[8 + j + k] + plane[8 + j - k]) + (
                        field[par, 8 + base + j, pl.ds(8 + 8 * t + k, 8), :]
                        + field[par, 8 + base + j, pl.ds(8 + 8 * t - k, 8), :]
                    )
                    total = total + F32(weights[k - 1]) * pairs
                here = plane[8 + j]
                total = total + F32(3.0 * centre) * here
                field[1 - par, 8 + base + j, rows, :] = (
                    2.0 * here
                    - field[1 - par, 8 + base + j, rows, :]
                    + speed[base + j, pl.ds(8 * t, 8), :] * total
                )

        @pl.when(c == 0)
        def _():
            at = (1 - par, 8 + rec_depth, pl.ds(8, span_x))
            field[at] = field[at] + surface[STEPS - 1 - n]

    def after(n, c):
        par = lax.rem(n, 2)
        base = layers * c
        each_end(x_ends, lambda side: x_copy(par, c, 1 - side, None).wait_recv())
        for side in range(2):
            t = (tiles - 1) * side
            for j in range(layers):
                total = jnp.zeros((8, span_y), F32)
                for k in range(1, 9):
                    start = k if side else 8 - k
                    total = total + F32(weights[k - 1]) * xin[par, c, side, j, pl.ds(start, 8), :]
                rows = pl.ds(8 + 8 * t, 8)
                field[1 - par, 8 + base + j, rows, :] = (
                    field[1 - par, 8 + base + j, rows, :]
                    + speed[base + j, pl.ds(8 * t, 8), :] * total
                )

    before(0, 0)

    def slot(s, carry):
        n, c = lax.div(s, SPLIT), lax.rem(s, SPLIT)
        nxt = 1 - lax.rem(n, 2)
        after(n, c)

        @pl.when(n < STEPS - 1)
        def _():
            each_end(x_ends, lambda side: x_copy(nxt, c, side, None).start())
            pack_y(nxt, c)
            each_end(y_ends, lambda side: y_copy(nxt, c, side).start())

        which = slot_ref[STEPS - 1 - n]
        zs = pl.ds(layers * c, layers)
        image[zs] = image[zs] + saved[which, zs] * (
            field[nxt, pl.ds(8 + layers * c, layers), pl.ds(8, span_x), :]
        )

        @pl.when(s + 1 < STEPS * SPLIT)
        def _():
            before(lax.div(s + 1, SPLIT), lax.rem(s + 1, SPLIT))

        return carry

    lax.fori_loop(0, STEPS * SPLIT, slot, 0)
    end = STEPS % 2
    result = pltpu.make_async_copy(
        field.at[end, pl.ds(8, depth), pl.ds(8, span_x), :], out_ref.at[0], load_sem.at[0]
    )
    result.start()

    sx = sx_ref[0].astype(F32)
    sy = sy_ref[0].astype(F32)
    cell_x = (tx * span_x + lax.broadcasted_iota(jnp.int32, (span_x, span_y), 0)).astype(F32) - sx
    cell_y = (ty * span_y + lax.broadcasted_iota(jnp.int32, (span_x, span_y), 1)).astype(F32) - sy
    flat = cell_x * cell_x + cell_y * cell_y

    def mute(z, carry):
        gap = z.astype(F32) - src_depth
        image[z] = image[z] * (1.0 - jnp.exp(-(gap * gap + flat) / (mute_radius * mute_radius)))
        return carry

    lax.fori_loop(0, depth, mute, 0)

    def piece(column_at, q):
        return pl.ds(8 * column_at + 2 * q, 2)

    def sum_far(q):
        return pltpu.make_async_remote_copy(
            src_ref=image.at[piece(opposite, q)],
            dst_ref=pass_in.at[q],
            send_sem=ra_send.at[q],
            recv_sem=ra_recv.at[q],
            device_id=to_right if q < 2 else to_left,
            device_id_type=MESH,
        )

    def sum_near(q, side):
        combined = (q < 2) == (side == 1)
        return pltpu.make_async_remote_copy(
            src_ref=pass_out.at[q] if combined else image.at[piece(right if side else left, q)],
            dst_ref=near_in.at[1 - side, q],
            send_sem=rb_send.at[q, side],
            recv_sem=rb_recv.at[q, 1 - side],
            device_id=to_right if side else to_left,
            device_id_type=MESH,
        )

    def sum_depth(distance):
        return pltpu.make_async_remote_copy(
            src_ref=part.at[zl_peer(distance)],
            dst_ref=last_in.at[distance - 1],
            send_sem=rd_send.at[distance - 1],
            recv_sem=rd_recv.at[distance - 1],
            device_id={"shot": col * 4 + zl_peer(distance)},
            device_id_type=MESH,
        )

    for q in range(4):
        sum_far(q).start()
    for q in range(4):
        sum_near(q, 0 if q < 2 else 1).start()
    for q in range(4):
        sum_far(q).wait_recv()
        pass_out[q] = pass_in[q] + image[piece(right if q < 2 else left, q)]
        sum_near(q, 1 if q < 2 else 0).start()
    for q in range(4):
        sum_near(q, 0).wait_recv()
        sum_near(q, 1).wait_recv()
        part[q] = image[piece(col, q)] + near_in[0, q] + near_in[1, q]
    for distance in (1, 2, 3):
        sum_depth(distance).start()
    total = part[zl]
    for distance in (1, 2, 3):
        sum_depth(distance).wait_recv()
        total = total + last_in[distance - 1]
    gradient = total * F32(1.0 / math.sqrt(lax.axis_size("shot") * STEPS))
    grad_ref[...] = gradient
    upd_ref[...] = model_ref[...] - step_size * gradient

    last = (STEPS - 1) % 2
    for c in range(SPLIT):
        each_end(x_ends, lambda side, c=c: x_copy(last, c, side, None).wait_send())
        each_end(y_ends, lambda side, c=c: y_copy(last, c, side).wait_send())
    for distance in (1, 2, 3):
        gather_z(distance).wait_send()
        sum_depth(distance).wait_send()
    for q in range(4):
        gather_relay(q).wait_send()
        sum_far(q).wait_send()
        for side in range(2):
            gather_x(q, side).wait_send()
            sum_near(q, side).wait_send()
    result.wait()


def shards(
    adjoint_prior,
    adjoint_now,
    forward_saved,
    residuals,
    receiver_x,
    receiver_y,
    source_x,
    source_y,
    saved_slot,
    model,
):
    _, depth, span_x, span_y = adjoint_now.shape
    layers = depth // SPLIT
    tiles = span_x // 8
    anywhere = pl.BlockSpec(memory_space=pl.ANY)
    vmem = pl.BlockSpec(memory_space=pltpu.VMEM)
    smem = pl.BlockSpec(memory_space=pltpu.SMEM)
    dma = pltpu.SemaphoreType.DMA
    return pl.pallas_call(
        kernel,
        out_shape=(
            jax.ShapeDtypeStruct(adjoint_now.shape, F32),
            jax.ShapeDtypeStruct(model.shape, F32),
            jax.ShapeDtypeStruct(model.shape, F32),
        ),
        in_specs=[anywhere, anywhere, anywhere, vmem, vmem, vmem, smem, smem, smem, vmem],
        out_specs=(anywhere, vmem, vmem),
        scratch_shapes=[
            pltpu.VMEM((2, depth + 16, span_x + 16, span_y), F32),
            pltpu.VMEM((depth, span_x, span_y), F32),
            pltpu.VMEM((2, depth, span_x, span_y), F32),
            pltpu.VMEM((depth, span_x, span_y), F32),
            pltpu.VMEM((STEPS, span_x, span_y), F32),
            pltpu.VMEM((layers, span_x, span_y), F32),
            pltpu.VMEM((512, 256), BF16),
            pltpu.VMEM((2, SPLIT, 2, layers, 16, span_y), F32),
            pltpu.VMEM((2, SPLIT, tiles, 8, span_y), F32),
            pltpu.VMEM((2, SPLIT, 2, tiles, 8, span_y), F32),
            pltpu.VMEM((4, 2, span_x, span_y), F32),
            pltpu.VMEM((4, 2, span_x, span_y), F32),
            pltpu.VMEM((2, 4, 2, span_x, span_y), F32),
            pltpu.VMEM((4, 2, span_x, span_y), F32),
            pltpu.VMEM((3, 2, span_x, span_y), F32),
            dma((4,)),
            dma((2, SPLIT, 2)),
            dma((2, SPLIT, 2)),
            dma((2, SPLIT, 2)),
            dma((2, SPLIT, 2)),
            dma((3,)),
            dma((3,)),
            dma((4, 2)),
            dma((4, 2)),
            dma((4,)),
            dma((4,)),
            dma((4,)),
            dma((4,)),
            dma((4, 2)),
            dma((4, 2)),
            dma((3,)),
            dma((3,)),
        ],
        compiler_params=pltpu.CompilerParams(
            collective_id=0, has_side_effects=True, vmem_limit_bytes=40 * 1024 * 1024
        ),
    )(
        adjoint_prior,
        adjoint_now,
        forward_saved,
        residuals,
        receiver_x,
        receiver_y,
        source_x,
        source_y,
        saved_slot,
        model,
    )


def solution(mesh):
    return jax.shard_map(
        shards,
        mesh=mesh,
        in_specs=(
            P("shot", None, "tx", "ty"),
            P("shot", None, "tx", "ty"),
            P("shot", None, None, "tx", "ty"),
            P("shot", None, None),
            P("shot", None),
            P("shot", None),
            P("shot"),
            P("shot"),
            P(),
            P("shot", "tx", "ty"),
        ),
        out_specs=(P("shot", None, "tx", "ty"), P("shot", "tx", "ty"), P("shot", "tx", "ty")),
        check_vma=False,
    )
```

```python
import math

import jax
import jax.numpy as jnp
from jax import lax
from jax.experimental import pallas as pl
from jax.experimental.pallas import tpu as pltpu
from jax.sharding import PartitionSpec as P

STEPS = 10
REACH = 8
SPLIT = 4

rec_depth = 2
src_depth = 3.0
mute_radius = 10.0
step_size = 0.01

MESH = pl.DeviceIdType.MESH
F32 = jnp.float32
BF16 = jnp.bfloat16


def coefficients():
    weights_table = []
    for offset in range(1, 9):
        weights_table.append(
            2.0
            * (-1.0) ** (offset + 1)
            * math.factorial(8) ** 2
            / (offset * offset * math.factorial(8 - offset) * math.factorial(8 + offset))
        )
    centre = -2.0 * sum(weights_table)
    return (centre, weights_table)


def halves(value):
    high = value.astype(BF16)
    low = (value - high.astype(F32)).astype(BF16)
    return high, low


def kernel(
    prior_ref,
    now_ref,
    fwd_ref,
    res_ref,
    rx_ref,
    ry_ref,
    sx_ref,
    sy_ref,
    slot_ref,
    model_ref,
    out_ref,
    sum_ref,
    field,
    speed,
    saved,
    image,
    surface,
    ylap,
    band,
    xin,
    yout,
    yin,
    pass_in,
    pass_out,
    near_in,
    part,
    last_in,
    load_sem,
    x_send,
    x_recv,
    y_send,
    y_recv,
    gz_send,
    gz_recv,
    gx_send,
    gx_recv,
    gr_send,
    gr_recv,
    ra_send,
    ra_recv,
    rb_send,
    rb_recv,
    rd_send,
    rd_recv,
):
    centre, weights = coefficients()
    depth, span_x, span_y = speed.shape
    layers = depth // SPLIT
    tiles = span_x // 8
    shot, tx, ty = lax.axis_index("shot"), lax.axis_index("tx"), lax.axis_index("ty")
    zl, col = lax.rem(shot, 4), lax.div(shot, 4)
    right, left = lax.rem(col + 1, 4), lax.rem(col + 3, 4)
    opposite = lax.rem(col + 2, 4)
    to_right = {"shot": right * 4 + zl}
    to_left = {"shot": left * 4 + zl}
    x_ends = ((tx > 0, {"tx": tx - 1}), (tx < lax.axis_size("tx") - 1, {"tx": tx + 1}))
    y_ends = ((ty > 0, {"ty": ty - 1}), (ty < lax.axis_size("ty") - 1, {"ty": ty + 1}))

    def zl_peer(distance):
        return lax.rem(zl + distance, 4)

    loads = [
        pltpu.make_async_copy(
            now_ref.at[0], field.at[0, pl.ds(8, depth), pl.ds(8, span_x), :], load_sem.at[0]
        ),
        pltpu.make_async_copy(
            prior_ref.at[0], field.at[1, pl.ds(8, depth), pl.ds(8, span_x), :], load_sem.at[1]
        ),
        pltpu.make_async_copy(fwd_ref.at[0], saved, load_sem.at[2]),
        pltpu.make_async_copy(model_ref, speed.at[pl.ds(2 * shot, 2)], load_sem.at[3]),
    ]
    for load in loads:
        load.start()

    xin[...] = jnp.zeros_like(xin)
    yin[...] = jnp.zeros_like(yin)

    barrier = pltpu.get_barrier_semaphore()
    for present, peer in x_ends + y_ends:

        @pl.when(present)
        def _(peer=peer):
            pl.semaphore_signal(barrier, inc=1, device_id=peer, device_id_type=MESH)

    for distance in (1, 2, 3):
        pl.semaphore_signal(
            barrier, inc=1, device_id={"shot": col * 4 + zl_peer(distance)}, device_id_type=MESH
        )
    for peer in (to_right, to_left):
        pl.semaphore_signal(barrier, inc=1, device_id=peer, device_id_type=MESH)
    for par in range(2):
        field[par, pl.ds(0, 8)] = jnp.zeros((8, span_x + 16, span_y), F32)
        field[par, pl.ds(depth + 8, 8)] = jnp.zeros((8, span_x + 16, span_y), F32)
        field[par, pl.ds(8, depth), pl.ds(0, 8)] = jnp.zeros((depth, 8, span_y), F32)
        field[par, pl.ds(8, depth), pl.ds(span_x + 8, 8)] = jnp.zeros((depth, 8, span_y), F32)
    neighbours = 5
    for present, _ in x_ends + y_ends:
        neighbours = neighbours + present.astype(jnp.int32)

    def gather_z(distance):
        return pltpu.make_async_remote_copy(
            src_ref=model_ref,
            dst_ref=speed.at[pl.ds(2 * shot, 2)],
            send_sem=gz_send.at[distance - 1],
            recv_sem=gz_recv.at[distance - 1],
            device_id={"shot": col * 4 + zl_peer(distance)},
            device_id_type=MESH,
        )

    def gather_x(block, side):
        where = pl.ds(2 * (col * 4 + zl_peer(4 - block)), 2)
        return pltpu.make_async_remote_copy(
            src_ref=model_ref if block == 0 else speed.at[where],
            dst_ref=speed.at[where],
            send_sem=gx_send.at[block, side],
            recv_sem=gx_recv.at[block, side],
            device_id=to_right if side else to_left,
            device_id_type=MESH,
        )

    def gather_relay(block):
        origin = left if block < 2 else right
        where = pl.ds(2 * (origin * 4 + zl_peer(4 - block)), 2)
        return pltpu.make_async_remote_copy(
            src_ref=speed.at[where],
            dst_ref=speed.at[where],
            send_sem=gr_send.at[block],
            recv_sem=gr_recv.at[block],
            device_id=to_right if block < 2 else to_left,
            device_id_type=MESH,
        )

    def x_copy(par, c, side, source):
        zs = pl.ds(layers * c, layers)
        if source is None:
            src = field.at[par, pl.ds(8 + layers * c, layers), pl.ds(8 + (span_x - 8) * side, 8), :]
        else:
            src = source.at[0, zs, pl.ds((span_x - 8) * side, 8), :]
        return pltpu.make_async_remote_copy(
            src_ref=src,
            dst_ref=xin.at[par, c, 1 - side, :, pl.ds(8 * (1 - side), 8), :],
            send_sem=x_send.at[par, c, side],
            recv_sem=x_recv.at[par, c, 1 - side],
            device_id=x_ends[side][1],
            device_id_type=MESH,
        )

    def y_copy(par, c, side):
        return pltpu.make_async_remote_copy(
            src_ref=yout.at[par, c],
            dst_ref=yin.at[par, c, 1 - side],
            send_sem=y_send.at[par, c, side],
            recv_sem=y_recv.at[par, c, 1 - side],
            device_id=y_ends[side][1],
            device_id_type=MESH,
        )

    def each_end(ends, action):
        for side in range(2):

            @pl.when(ends[side][0])
            def _(side=side):
                action(side)

    lane = lax.broadcasted_iota(jnp.int32, (8, span_y), 1)
    group = lax.div(lane, 16)
    from_left = lax.rem(lane, 16) < 8

    def pack_y(par, c):
        for t in range(tiles):
            packed = jnp.zeros((8, span_y), F32)
            for j in range(layers):
                value = field[par, 8 + layers * c + j, pl.ds(8 + 8 * t, 8), :]
                packed = jnp.where(group == j, pltpu.roll(value, (16 * j + 8) % span_y, 1), packed)
            yout[par, c, t] = packed

    loads[0].wait()
    for c in range(SPLIT):
        pack_y(0, c)
    pl.semaphore_wait(barrier, neighbours)
    for distance in (1, 2, 3):
        gather_z(distance).start()
    for side in range(2):
        gather_x(0, side).start()
    for c in range(SPLIT):
        each_end(x_ends, lambda side, c=c: x_copy(0, c, side, now_ref).start())
    for c in range(SPLIT):
        each_end(y_ends, lambda side, c=c: y_copy(0, c, side).start())

    row = lax.broadcasted_iota(jnp.int32, (span_y, span_y), 0)
    column = lax.broadcasted_iota(jnp.int32, (span_y, span_y), 1)
    away = jnp.abs(row - column)
    inner = lax.rem(row, 16)
    halo_away = jnp.where(inner < 8, column + 8 - inner, span_y - 8 + inner - column)
    own = jnp.zeros((span_y, span_y), F32)
    edge = jnp.zeros((span_y, span_y), F32)
    for k in range(1, 9):
        own = jnp.where(away == k, F32(weights[k - 1]), own)
        edge = jnp.where(halo_away == k, F32(weights[k - 1]), edge)
    for i, matrix in enumerate((own, edge)):
        high, low = halves(matrix)
        band[pl.ds(256 * i, 128), pl.ds(0, 128)] = high
        band[pl.ds(256 * i, 128), pl.ds(128, 128)] = low
        band[pl.ds(256 * i + 128, 128), pl.ds(0, 128)] = high
        band[pl.ds(256 * i + 128, 128), pl.ds(128, 128)] = jnp.zeros((128, 128), BF16)

    count = rx_ref.shape[1]
    local_x = rx_ref[...] - tx * span_x
    local_y = ry_ref[...] - ty * span_y
    at_x = local_x == lax.broadcasted_iota(jnp.int32, (span_x, count), 0)
    at_y = (local_y == lax.broadcasted_iota(jnp.int32, (span_y, count), 0)).astype(F32).astype(BF16)

    def spread(moment, carry):
        traces = jnp.where(at_x, res_ref[moment], 0.0)
        high = traces.astype(BF16)
        rest = traces - high.astype(F32)
        mid = rest.astype(BF16)
        low = (rest - mid.astype(F32)).astype(BF16)
        total = jnp.zeros((span_x, span_y), F32)
        for term in (low, mid, high):
            total = total + lax.dot_general(
                term, at_y, (((1,), (1,)), ((), ())), preferred_element_type=F32
            )
        surface[moment] = total
        return carry

    lax.fori_loop(0, STEPS, spread, 0)

    def chunk_at(place):
        return lax.rem(col + (2, 1, 3, 0)[place], SPLIT)

    def chunk_of(place):
        return lax.rem(col + 2 + 3 * place + 3 * lax.div(place * (place - 1), 2), SPLIT)

    def stencil(par, c, store):
        base = layers * c
        value = field[par, pl.ds(8 + base, layers), pl.ds(8, span_x), :].reshape(
            layers * span_x, span_y
        )
        high, low = halves(value)
        halo = []
        for t in range(tiles):
            halo.append(jnp.where(from_left, yin[par, c, 0, t], yin[par, c, 1, t]))
        halo = jnp.concatenate(halo, axis=0)
        groups = lax.div(lax.broadcasted_iota(jnp.int32, (span_x, span_y), 1), 16)
        halo = jnp.concatenate([jnp.where(groups == j, halo, 0.0) for j in range(layers)], axis=0)
        halo_high, halo_low = halves(halo)
        sides = jnp.dot(
            jnp.concatenate([high, low, halo_high, halo_low], axis=1),
            band[...],
            preferred_element_type=F32,
        )
        ylap[...] = (sides[:, :span_y] + sides[:, span_y:]).reshape(layers, span_x, span_y)
        for t in range(tiles):
            rows = pl.ds(8 + 8 * t, 8)
            plane = [field[par, base + i, rows, :] for i in range(layers + 16)]
            made = []
            for j in range(layers):
                total = ylap[j, pl.ds(8 * t, 8), :]
                for k in range(1, 9):
                    pairs = (plane[8 + j + k] + plane[8 + j - k]) + (
                        field[par, 8 + base + j, pl.ds(8 + 8 * t + k, 8), :]
                        + field[par, 8 + base + j, pl.ds(8 + 8 * t - k, 8), :]
                    )
                    total = total + F32(weights[k - 1]) * pairs
                here = plane[8 + j]
                made.append((here, total + F32(3.0 * centre) * here))
            store(t, made)

    def add_receivers(n, c):
        @pl.when(c == 0)
        def _():
            at = (1 - lax.rem(n, 2), 8 + rec_depth, pl.ds(8, span_x))
            field[at] = field[at] + surface[STEPS - 1 - n]

    def before(n, c):
        par = lax.rem(n, 2)
        each_end(x_ends, lambda side: x_copy(1 - par, c, side, None).wait_send())
        each_end(y_ends, lambda side: y_copy(1 - par, c, side).wait_send())
        each_end(y_ends, lambda side: y_copy(par, c, 1 - side).wait_recv())
        base = layers * c

        def store(t, made):
            rows = pl.ds(8 + 8 * t, 8)
            new = [
                2.0 * here
                - field[1 - par, 8 + base + j, rows, :]
                + speed[base + j, pl.ds(8 * t, 8), :] * total
                for j, (here, total) in enumerate(made)
            ]
            for j in range(layers):
                field[1 - par, 8 + base + j, rows, :] = new[j]

        stencil(par, c, store)
        add_receivers(n, c)

    def before_first(c):
        each_end(y_ends, lambda side: y_copy(0, c, 1 - side).wait_recv())
        base = layers * c

        def store(t, made):
            for j in range(layers):
                image[base + j, pl.ds(8 * t, 8), :] = made[j][1]

        stencil(0, c, store)

    def finish_first(c):
        zs = pl.ds(layers * c, layers)
        inside = (pl.ds(8 + layers * c, layers), pl.ds(8, span_x))
        field[(1,) + inside] = (
            2.0 * field[(0,) + inside] - field[(1,) + inside] + speed[zs] * image[zs]
        )
        add_receivers(0, c)

    def after(n, c):
        par = lax.rem(n, 2)
        base = layers * c
        each_end(x_ends, lambda side: x_copy(par, c, 1 - side, None).wait_recv())
        for side in range(2):
            t = (tiles - 1) * side
            rows = pl.ds(8 + 8 * t, 8)
            new = []
            for j in range(layers):
                total = jnp.zeros((8, span_y), F32)
                for k in range(1, 9):
                    start = k if side else 8 - k
                    total = total + F32(weights[k - 1]) * xin[par, c, side, j, pl.ds(start, 8), :]
                new.append(
                    field[1 - par, 8 + base + j, rows, :]
                    + speed[base + j, pl.ds(8 * t, 8), :] * total
                )
            for j in range(layers):
                field[1 - par, 8 + base + j, rows, :] = new[j]

    def send(n, c):
        nxt = 1 - lax.rem(n, 2)
        each_end(x_ends, lambda side: x_copy(nxt, c, side, None).start())
        pack_y(nxt, c)
        each_end(y_ends, lambda side: y_copy(nxt, c, side).start())

    def imaged(n, c):
        zs = pl.ds(layers * c, layers)
        inside = (1 - lax.rem(n, 2), pl.ds(8 + layers * c, layers), pl.ds(8, span_x))
        return saved[slot_ref[STEPS - 1 - n], zs] * field[inside]

    for block in (1, 2, 3):
        gather_z(block).wait_recv()
        for side in range(2):
            gather_x(block, side).start()
    for place in (0, 1):
        before_first(chunk_at(place))
    for block in range(4):
        gather_x(block, 1).wait_recv()
        if block < 2:
            gather_relay(block).start()
        gather_x(block, 0).wait_recv()
        if block >= 2:
            gather_relay(block).start()
    for place in (2, 3):
        before_first(chunk_at(place))
    loads[1].wait()
    for block in range(4):
        gather_relay(block).wait_recv()
    loads[3].wait()

    for place in range(SPLIT):
        c = chunk_at(place)
        finish_first(c)
        after(0, c)
        send(0, c)
        if place == 0:
            loads[2].wait()
        image[pl.ds(layers * c, layers)] = imaged(0, c)
    before(1, chunk_at(0))

    def slot(s, carry):
        n, c = lax.div(s, SPLIT), chunk_of(lax.rem(s, SPLIT))
        after(n, c)
        send(n, c)
        zs = pl.ds(layers * c, layers)
        image[zs] = image[zs] + imaged(n, c)
        before(lax.div(s + 1, SPLIT), chunk_of(lax.rem(s + 1, SPLIT)))
        return carry

    lax.fori_loop(SPLIT, (STEPS - 1) * SPLIT, slot, 0)

    sx = sx_ref[0].astype(F32)
    sy = sy_ref[0].astype(F32)
    cell_x = (tx * span_x + lax.broadcasted_iota(jnp.int32, (span_x, span_y), 0)).astype(F32) - sx
    cell_y = (ty * span_y + lax.broadcasted_iota(jnp.int32, (span_x, span_y), 1)).astype(F32) - sy
    flat = cell_x * cell_x + cell_y * cell_y

    def piece(column_at, q):
        return pl.ds(8 * column_at + 2 * q, 2)

    def sum_far(q):
        return pltpu.make_async_remote_copy(
            src_ref=image.at[piece(opposite, q)],
            dst_ref=pass_in.at[q],
            send_sem=ra_send.at[q],
            recv_sem=ra_recv.at[q],
            device_id=to_right if q < 2 else to_left,
            device_id_type=MESH,
        )

    def sum_near(q, side):
        combined = (q < 2) == (side == 1)
        return pltpu.make_async_remote_copy(
            src_ref=pass_out.at[q] if combined else image.at[piece(right if side else left, q)],
            dst_ref=near_in.at[1 - side, q],
            send_sem=rb_send.at[q, side],
            recv_sem=rb_recv.at[q, 1 - side],
            device_id=to_right if side else to_left,
            device_id_type=MESH,
        )

    def sum_depth(distance):
        return pltpu.make_async_remote_copy(
            src_ref=part.at[zl_peer(distance)],
            dst_ref=last_in.at[distance - 1],
            send_sem=rd_send.at[distance - 1],
            recv_sem=rd_recv.at[distance - 1],
            device_id={"shot": col * 4 + zl_peer(distance)},
            device_id_type=MESH,
        )

    results = []
    for place in range(SPLIT):
        c = chunk_at(place)
        after(STEPS - 1, c)
        zs = pl.ds(layers * c, layers)
        muted = image[zs] + imaged(STEPS - 1, c)
        for j in range(layers):
            gap = (layers * c + j).astype(F32) - src_depth
            image[layers * c + j] = muted[j] * (
                1.0 - jnp.exp(-(gap * gap + flat) / (mute_radius * mute_radius))
            )
        result = pltpu.make_async_copy(
            field.at[STEPS % 2, pl.ds(8 + layers * c, layers), pl.ds(8, span_x), :],
            out_ref.at[0, zs],
            load_sem.at[place],
        )
        result.start()
        results.append(result)
        if place == 0:
            for q in range(4):
                sum_far(q).start()
        if place == 1:
            for q in (2, 3):
                sum_near(q, 1).start()
        if place == 2:
            for q in (0, 1):
                sum_near(q, 0).start()
            for q in (0, 1):
                sum_far(q).wait_recv()
                pass_out[q] = pass_in[q] + image[piece(right, q)]
            for q in (0, 1):
                sum_near(q, 1).start()
        if place < SPLIT - 1:
            before(STEPS - 1, chunk_at(place + 1))
        if place == 2:
            for q in (2, 3):
                sum_far(q).wait_recv()
                pass_out[q] = pass_in[q] + image[piece(left, q)]
            for q in (2, 3):
                sum_near(q, 0).start()
    for q in range(4):
        sum_near(q, 0).wait_recv()
        sum_near(q, 1).wait_recv()
        part[q] = image[piece(col, q)] + near_in[0, q] + near_in[1, q]
    for distance in (1, 2, 3):
        sum_depth(distance).start()
    total = part[zl]
    for distance in (1, 2, 3):
        sum_depth(distance).wait_recv()
        total = total + last_in[distance - 1]
    sum_ref[...] = total

    last = (STEPS - 1) % 2
    for c in range(SPLIT):
        each_end(x_ends, lambda side, c=c: x_copy(last, c, side, None).wait_send())
        each_end(y_ends, lambda side, c=c: y_copy(last, c, side).wait_send())
    for distance in (1, 2, 3):
        gather_z(distance).wait_send()
        sum_depth(distance).wait_send()
    for q in range(4):
        gather_relay(q).wait_send()
        sum_far(q).wait_send()
        for side in range(2):
            gather_x(q, side).wait_send()
            sum_near(q, side).wait_send()
    for result in results:
        result.wait()


def shards(
    adjoint_prior,
    adjoint_now,
    forward_saved,
    residuals,
    receiver_x,
    receiver_y,
    source_x,
    source_y,
    saved_slot,
    model,
):
    _, depth, span_x, span_y = adjoint_now.shape
    layers = depth // SPLIT
    tiles = span_x // 8
    anywhere = pl.BlockSpec(memory_space=pl.ANY)
    vmem = pl.BlockSpec(memory_space=pltpu.VMEM)
    smem = pl.BlockSpec(memory_space=pltpu.SMEM)
    dma = pltpu.SemaphoreType.DMA
    state, summed = pl.pallas_call(
        kernel,
        out_shape=(
            jax.ShapeDtypeStruct(adjoint_now.shape, F32),
            jax.ShapeDtypeStruct(model.shape, F32),
        ),
        in_specs=[anywhere, anywhere, anywhere, vmem, vmem, vmem, smem, smem, smem, vmem],
        out_specs=(anywhere, vmem),
        scratch_shapes=[
            pltpu.VMEM((2, depth + 16, span_x + 16, span_y), F32),
            pltpu.VMEM((depth, span_x, span_y), F32),
            pltpu.VMEM((2, depth, span_x, span_y), F32),
            pltpu.VMEM((depth, span_x, span_y), F32),
            pltpu.VMEM((STEPS, span_x, span_y), F32),
            pltpu.VMEM((layers, span_x, span_y), F32),
            pltpu.VMEM((512, 256), BF16),
            pltpu.VMEM((2, SPLIT, 2, layers, 16, span_y), F32),
            pltpu.VMEM((2, SPLIT, tiles, 8, span_y), F32),
            pltpu.VMEM((2, SPLIT, 2, tiles, 8, span_y), F32),
            pltpu.VMEM((4, 2, span_x, span_y), F32),
            pltpu.VMEM((4, 2, span_x, span_y), F32),
            pltpu.VMEM((2, 4, 2, span_x, span_y), F32),
            pltpu.VMEM((4, 2, span_x, span_y), F32),
            pltpu.VMEM((3, 2, span_x, span_y), F32),
            dma((4,)),
            dma((2, SPLIT, 2)),
            dma((2, SPLIT, 2)),
            dma((2, SPLIT, 2)),
            dma((2, SPLIT, 2)),
            dma((3,)),
            dma((3,)),
            dma((4, 2)),
            dma((4, 2)),
            dma((4,)),
            dma((4,)),
            dma((4,)),
            dma((4,)),
            dma((4, 2)),
            dma((4, 2)),
            dma((3,)),
            dma((3,)),
        ],
        compiler_params=pltpu.CompilerParams(
            collective_id=0, has_side_effects=True, vmem_limit_bytes=63 * 1024 * 1024
        ),
    )(
        adjoint_prior,
        adjoint_now,
        forward_saved,
        jnp.swapaxes(residuals, 0, 1),
        receiver_x,
        receiver_y,
        source_x,
        source_y,
        saved_slot,
        model,
    )
    gradient = summed * (1.0 / math.sqrt(lax.axis_size("shot") * STEPS))
    return state, gradient, model - step_size * gradient


def solution(mesh):
    return jax.shard_map(
        shards,
        mesh=mesh,
        in_specs=(
            P("shot", None, "tx", "ty"),
            P("shot", None, "tx", "ty"),
            P("shot", None, None, "tx", "ty"),
            P("shot", None, None),
            P("shot", None),
            P("shot", None),
            P("shot"),
            P("shot"),
            P(),
            P("shot", "tx", "ty"),
        ),
        out_specs=(P("shot", None, "tx", "ty"), P("shot", "tx", "ty"), P("shot", "tx", "ty")),
        check_vma=False,
    )
```

```python
import math

import jax
import jax.numpy as jnp
from jax import lax
from jax.experimental import pallas as pl
from jax.experimental.pallas import tpu as pltpu
from jax.sharding import PartitionSpec as P

STEPS = 10
REACH = 8
SPLIT = 4

rec_depth = 2
src_depth = 3.0
mute_radius = 10.0
step_size = 0.01

MESH = pl.DeviceIdType.MESH
F32 = jnp.float32
BF16 = jnp.bfloat16


def coefficients():
    weights_table = []
    for offset in range(1, 9):
        weights_table.append(
            2.0
            * (-1.0) ** (offset + 1)
            * math.factorial(8) ** 2
            / (offset * offset * math.factorial(8 - offset) * math.factorial(8 + offset))
        )
    centre = -2.0 * sum(weights_table)
    return (centre, weights_table)


def halves(value):
    high = value.astype(BF16)
    low = (value - high.astype(F32)).astype(BF16)
    return high, low


def kernel(
    prior_ref,
    now_ref,
    fwd_ref,
    res_ref,
    rx_ref,
    ry_ref,
    sx_ref,
    sy_ref,
    slot_ref,
    model_ref,
    out_ref,
    sum_ref,
    field,
    speed,
    saved,
    image,
    surface,
    ylap,
    band,
    comb,
    xin,
    yout,
    yin,
    pass_in,
    pass_out,
    near_in,
    part,
    last_in,
    load_sem,
    x_send,
    x_recv,
    y_send,
    y_recv,
    gz_send,
    gz_recv,
    gx_send,
    gx_recv,
    gr_send,
    gr_recv,
    ra_send,
    ra_recv,
    rb_send,
    rb_recv,
    rd_send,
    rd_recv,
):
    centre, weights = coefficients()
    depth, span_x, span_y = speed.shape
    layers = depth // SPLIT
    tiles = span_x // 8
    shot, tx, ty = lax.axis_index("shot"), lax.axis_index("tx"), lax.axis_index("ty")
    zl, col = lax.rem(shot, 4), lax.div(shot, 4)
    right, left = lax.rem(col + 1, 4), lax.rem(col + 3, 4)
    opposite = lax.rem(col + 2, 4)
    to_right = {"shot": right * 4 + zl}
    to_left = {"shot": left * 4 + zl}
    x_ends = ((tx > 0, {"tx": tx - 1}), (tx < lax.axis_size("tx") - 1, {"tx": tx + 1}))
    y_ends = ((ty > 0, {"ty": ty - 1}), (ty < lax.axis_size("ty") - 1, {"ty": ty + 1}))

    def zl_peer(distance):
        return lax.rem(zl + distance, 4)

    loads = [
        pltpu.make_async_copy(
            now_ref.at[0], field.at[0, pl.ds(8, depth), pl.ds(8, span_x), :], load_sem.at[0]
        ),
        pltpu.make_async_copy(
            prior_ref.at[0], field.at[1, pl.ds(8, depth), pl.ds(8, span_x), :], load_sem.at[1]
        ),
        pltpu.make_async_copy(fwd_ref.at[0], saved, load_sem.at[2]),
        pltpu.make_async_copy(model_ref, speed.at[pl.ds(2 * shot, 2)], load_sem.at[3]),
    ]
    for load in loads:
        load.start()

    xin[...] = jnp.zeros_like(xin)
    yin[...] = jnp.zeros_like(yin)

    barrier = pltpu.get_barrier_semaphore()
    for present, peer in x_ends + y_ends:

        @pl.when(present)
        def _(peer=peer):
            pl.semaphore_signal(barrier, inc=1, device_id=peer, device_id_type=MESH)

    for distance in (1, 2, 3):
        pl.semaphore_signal(
            barrier, inc=1, device_id={"shot": col * 4 + zl_peer(distance)}, device_id_type=MESH
        )
    for peer in (to_right, to_left):
        pl.semaphore_signal(barrier, inc=1, device_id=peer, device_id_type=MESH)
    for par in range(2):
        field[par, pl.ds(0, 8)] = jnp.zeros((8, span_x + 16, span_y), F32)
        field[par, pl.ds(depth + 8, 8)] = jnp.zeros((8, span_x + 16, span_y), F32)
        field[par, pl.ds(8, depth), pl.ds(0, 8)] = jnp.zeros((depth, 8, span_y), F32)
        field[par, pl.ds(8, depth), pl.ds(span_x + 8, 8)] = jnp.zeros((depth, 8, span_y), F32)
    neighbours = 5
    for present, _ in x_ends + y_ends:
        neighbours = neighbours + present.astype(jnp.int32)

    def gather_z(distance):
        return pltpu.make_async_remote_copy(
            src_ref=model_ref,
            dst_ref=speed.at[pl.ds(2 * shot, 2)],
            send_sem=gz_send.at[distance - 1],
            recv_sem=gz_recv.at[distance - 1],
            device_id={"shot": col * 4 + zl_peer(distance)},
            device_id_type=MESH,
        )

    def gather_x(block, side):
        where = pl.ds(2 * (col * 4 + zl_peer(4 - block)), 2)
        return pltpu.make_async_remote_copy(
            src_ref=model_ref if block == 0 else speed.at[where],
            dst_ref=speed.at[where],
            send_sem=gx_send.at[block, side],
            recv_sem=gx_recv.at[block, side],
            device_id=to_right if side else to_left,
            device_id_type=MESH,
        )

    def gather_relay(block):
        origin = left if block < 2 else right
        where = pl.ds(2 * (origin * 4 + zl_peer(4 - block)), 2)
        return pltpu.make_async_remote_copy(
            src_ref=speed.at[where],
            dst_ref=speed.at[where],
            send_sem=gr_send.at[block],
            recv_sem=gr_recv.at[block],
            device_id=to_right if block < 2 else to_left,
            device_id_type=MESH,
        )

    def x_copy(par, c, side, source):
        zs = pl.ds(layers * c, layers)
        if source is None:
            src = field.at[par, pl.ds(8 + layers * c, layers), pl.ds(8 + (span_x - 8) * side, 8), :]
        else:
            src = source.at[0, zs, pl.ds((span_x - 8) * side, 8), :]
        return pltpu.make_async_remote_copy(
            src_ref=src,
            dst_ref=xin.at[par, c, 1 - side, :, pl.ds(8 * (1 - side), 8), :],
            send_sem=x_send.at[par, c, side],
            recv_sem=x_recv.at[par, c, 1 - side],
            device_id=x_ends[side][1],
            device_id_type=MESH,
        )

    def y_copy(par, c, side):
        return pltpu.make_async_remote_copy(
            src_ref=yout.at[par, c],
            dst_ref=yin.at[par, c, 1 - side],
            send_sem=y_send.at[par, c, side],
            recv_sem=y_recv.at[par, c, 1 - side],
            device_id=y_ends[side][1],
            device_id_type=MESH,
        )

    def each_end(ends, action):
        for side in range(2):

            @pl.when(ends[side][0])
            def _(side=side):
                action(side)

    lane = lax.broadcasted_iota(jnp.int32, (8, span_y), 1)
    group = lax.div(lane, 16)
    from_left = lax.rem(lane, 16) < 8

    def pack_y(par, c):
        for t in range(tiles):
            packed = jnp.zeros((8, span_y), F32)
            for j in range(layers):
                value = field[par, 8 + layers * c + j, pl.ds(8 + 8 * t, 8), :]
                packed = jnp.where(group == j, pltpu.roll(value, (16 * j + 8) % span_y, 1), packed)
            yout[par, c, t] = packed

    loads[0].wait()
    for c in range(SPLIT):
        pack_y(0, c)
    pl.semaphore_wait(barrier, neighbours)
    for distance in (1, 2, 3):
        gather_z(distance).start()
    for side in range(2):
        gather_x(0, side).start()
    for c in range(SPLIT):
        each_end(x_ends, lambda side, c=c: x_copy(0, c, side, now_ref).start())
    for c in range(SPLIT):
        each_end(y_ends, lambda side, c=c: y_copy(0, c, side).start())

    row = lax.broadcasted_iota(jnp.int32, (span_y, span_y), 0)
    column = lax.broadcasted_iota(jnp.int32, (span_y, span_y), 1)
    away = jnp.abs(row - column)
    inner = lax.rem(row, 16)
    halo_away = jnp.where(inner < 8, column + 8 - inner, span_y - 8 + inner - column)
    own = jnp.zeros((span_y, span_y), F32)
    edge = jnp.zeros((span_y, span_y), F32)
    for k in range(1, 9):
        own = jnp.where(away == k, F32(weights[k - 1]), own)
        edge = jnp.where(halo_away == k, F32(weights[k - 1]), edge)
    for i, matrix in enumerate((own, edge)):
        high, low = halves(matrix)
        band[pl.ds(256 * i, 128), pl.ds(0, 128)] = high
        band[pl.ds(256 * i, 128), pl.ds(128, 128)] = low
        band[pl.ds(256 * i + 128, 128), pl.ds(0, 128)] = high
        band[pl.ds(256 * i + 128, 128), pl.ds(128, 128)] = jnp.zeros((128, 128), BF16)

    cells = layers * span_x
    row = lax.broadcasted_iota(jnp.int32, (cells, cells), 0)
    column = lax.broadcasted_iota(jnp.int32, (cells, cells), 1)
    away = jnp.where(lax.div(row, span_x) == lax.div(column, span_x), jnp.abs(row - column), 0)
    inner = jnp.zeros((cells, cells), F32)
    for k in range(1, 9):
        inner = jnp.where(away == k, F32(weights[k - 1]), inner)
    comb[0], comb[1] = halves(inner)

    count = rx_ref.shape[1]
    local_x = rx_ref[...] - tx * span_x
    local_y = ry_ref[...] - ty * span_y
    at_x = local_x == lax.broadcasted_iota(jnp.int32, (span_x, count), 0)
    at_y = (local_y == lax.broadcasted_iota(jnp.int32, (span_y, count), 0)).astype(F32).astype(BF16)

    def spread(moment, carry):
        traces = jnp.where(at_x, res_ref[moment], 0.0)
        high = traces.astype(BF16)
        rest = traces - high.astype(F32)
        mid = rest.astype(BF16)
        low = (rest - mid.astype(F32)).astype(BF16)
        total = jnp.zeros((span_x, span_y), F32)
        for term in (low, mid, high):
            total = total + lax.dot_general(
                term, at_y, (((1,), (1,)), ((), ())), preferred_element_type=F32
            )
        surface[moment] = total
        return carry

    lax.fori_loop(0, STEPS, spread, 0)

    def chunk_at(place):
        return lax.rem(col + (2, 1, 3, 0)[place], SPLIT)

    def stencil(par, c, store):
        base = layers * c
        value = field[par, pl.ds(8 + base, layers), pl.ds(8, span_x), :].reshape(
            layers * span_x, span_y
        )
        high, low = halves(value)
        halo = []
        for t in range(tiles):
            halo.append(jnp.where(from_left, yin[par, c, 0, t], yin[par, c, 1, t]))
        halo = jnp.concatenate(halo, axis=0)
        groups = lax.div(lax.broadcasted_iota(jnp.int32, (span_x, span_y), 1), 16)
        halo = jnp.concatenate([jnp.where(groups == j, halo, 0.0) for j in range(layers)], axis=0)
        halo_high, halo_low = halves(halo)
        sides = jnp.dot(
            jnp.concatenate([high, low, halo_high, halo_low], axis=1),
            band[...],
            preferred_element_type=F32,
        )
        across = jnp.dot(
            comb[0], jnp.concatenate([high, low], axis=1), preferred_element_type=F32
        )
        across_low = jnp.dot(comb[1], high, preferred_element_type=F32)
        both = sides + across
        ylap[...] = (both[:, :span_y] + both[:, span_y:] + across_low).reshape(
            layers, span_x, span_y
        )
        for t in range(tiles):
            rows = pl.ds(8 + 8 * t, 8)
            plane = [field[par, base + i, rows, :] for i in range(layers + 16)]
            made = []
            for j in range(layers):
                here = plane[8 + j]
                total = F32(3.0 * centre) * here
                for k in range(1, 9):
                    pairs = plane[8 + j + k] + plane[8 + j - k]
                    total = total + F32(weights[k - 1]) * pairs
                made.append((here, total + ylap[j, pl.ds(8 * t, 8), :]))
            store(t, made)

    def add_receivers(n, c, par):
        @pl.when(c == 0)
        def _():
            at = (1 - par, 8 + rec_depth, pl.ds(8, span_x))
            field[at] = field[at] + surface[STEPS - 1 - n]

    def before(n, c, par):
        each_end(x_ends, lambda side: x_copy(1 - par, c, side, None).wait_send())
        each_end(y_ends, lambda side: y_copy(1 - par, c, side).wait_send())
        each_end(y_ends, lambda side: y_copy(par, c, 1 - side).wait_recv())
        base = layers * c

        def store(t, made):
            rows = pl.ds(8 + 8 * t, 8)
            new = [
                2.0 * here
                - field[1 - par, 8 + base + j, rows, :]
                + speed[base + j, pl.ds(8 * t, 8), :] * total
                for j, (here, total) in enumerate(made)
            ]
            for j in range(layers):
                field[1 - par, 8 + base + j, rows, :] = new[j]

        stencil(par, c, store)
        add_receivers(n, c, par)

    def before_first(c):
        each_end(y_ends, lambda side: y_copy(0, c, 1 - side).wait_recv())
        base = layers * c

        def store(t, made):
            for j in range(layers):
                image[base + j, pl.ds(8 * t, 8), :] = made[j][1]

        stencil(0, c, store)

    def finish_first(c):
        zs = pl.ds(layers * c, layers)
        inside = (pl.ds(8 + layers * c, layers), pl.ds(8, span_x))
        field[(1,) + inside] = (
            2.0 * field[(0,) + inside] - field[(1,) + inside] + speed[zs] * image[zs]
        )
        add_receivers(0, c, 0)

    def after(c, par):
        base = layers * c
        each_end(x_ends, lambda side: x_copy(par, c, 1 - side, None).wait_recv())
        for side in range(2):
            t = (tiles - 1) * side
            rows = pl.ds(8 + 8 * t, 8)
            new = []
            for j in range(layers):
                total = jnp.zeros((8, span_y), F32)
                for k in range(1, 9):
                    start = k if side else 8 - k
                    total = total + F32(weights[k - 1]) * xin[par, c, side, j, pl.ds(start, 8), :]
                new.append(
                    field[1 - par, 8 + base + j, rows, :]
                    + speed[base + j, pl.ds(8 * t, 8), :] * total
                )
            for j in range(layers):
                field[1 - par, 8 + base + j, rows, :] = new[j]

    def send(c, nxt):
        each_end(x_ends, lambda side: x_copy(nxt, c, side, None).start())
        pack_y(nxt, c)
        each_end(y_ends, lambda side: y_copy(nxt, c, side).start())

    def imaged(n, c, nxt):
        zs = pl.ds(layers * c, layers)
        inside = (nxt, pl.ds(8 + layers * c, layers), pl.ds(8, span_x))
        return saved[slot_ref[STEPS - 1 - n], zs] * field[inside]

    for block in (1, 2, 3):
        gather_z(block).wait_recv()
        for side in range(2):
            gather_x(block, side).start()
    for place in (0, 1):
        before_first(chunk_at(place))
    for block in range(4):
        gather_x(block, 1).wait_recv()
        if block < 2:
            gather_relay(block).start()
        gather_x(block, 0).wait_recv()
        if block >= 2:
            gather_relay(block).start()
    for place in (2, 3):
        before_first(chunk_at(place))
    loads[1].wait()
    for block in range(4):
        gather_relay(block).wait_recv()
    loads[3].wait()

    for place in range(SPLIT):
        c = chunk_at(place)
        finish_first(c)
        after(c, 0)
        send(c, 1)
        if place == 0:
            loads[2].wait()
        image[pl.ds(layers * c, layers)] = imaged(0, c, 1)
    before(1, chunk_at(0), 1)

    def two_steps(pair, carry):
        for half in range(2):
            n = 1 + 2 * pair + half
            par = 1 - half
            for place in range(SPLIT):
                c = chunk_at(place)
                after(c, par)
                send(c, 1 - par)
                zs = pl.ds(layers * c, layers)
                image[zs] = image[zs] + imaged(n, c, 1 - par)
                if place < SPLIT - 1:
                    before(n, chunk_at(place + 1), par)
                else:
                    before(n + 1, chunk_at(0), 1 - par)
        return carry

    lax.fori_loop(0, (STEPS - 2) // 2, two_steps, 0)

    sx = sx_ref[0].astype(F32)
    sy = sy_ref[0].astype(F32)
    cell_x = (tx * span_x + lax.broadcasted_iota(jnp.int32, (span_x, span_y), 0)).astype(F32) - sx
    cell_y = (ty * span_y + lax.broadcasted_iota(jnp.int32, (span_x, span_y), 1)).astype(F32) - sy
    flat = cell_x * cell_x + cell_y * cell_y

    def piece(column_at, q):
        return pl.ds(8 * column_at + 2 * q, 2)

    def sum_far(q):
        return pltpu.make_async_remote_copy(
            src_ref=image.at[piece(opposite, q)],
            dst_ref=pass_in.at[q],
            send_sem=ra_send.at[q],
            recv_sem=ra_recv.at[q],
            device_id=to_right if q < 2 else to_left,
            device_id_type=MESH,
        )

    def sum_near(q, side):
        combined = (q < 2) == (side == 1)
        return pltpu.make_async_remote_copy(
            src_ref=pass_out.at[q] if combined else image.at[piece(right if side else left, q)],
            dst_ref=near_in.at[1 - side, q],
            send_sem=rb_send.at[q, side],
            recv_sem=rb_recv.at[q, 1 - side],
            device_id=to_right if side else to_left,
            device_id_type=MESH,
        )

    def sum_depth(distance):
        return pltpu.make_async_remote_copy(
            src_ref=part.at[zl_peer(distance)],
            dst_ref=last_in.at[distance - 1],
            send_sem=rd_send.at[distance - 1],
            recv_sem=rd_recv.at[distance - 1],
            device_id={"shot": col * 4 + zl_peer(distance)},
            device_id_type=MESH,
        )

    results = []
    for place in range(SPLIT):
        c = chunk_at(place)
        after(c, (STEPS - 1) % 2)
        zs = pl.ds(layers * c, layers)
        muted = image[zs] + imaged(STEPS - 1, c, STEPS % 2)
        for j in range(layers):
            gap = (layers * c + j).astype(F32) - src_depth
            image[layers * c + j] = muted[j] * (
                1.0 - jnp.exp(-(gap * gap + flat) / (mute_radius * mute_radius))
            )
        result = pltpu.make_async_copy(
            field.at[STEPS % 2, pl.ds(8 + layers * c, layers), pl.ds(8, span_x), :],
            out_ref.at[0, zs],
            load_sem.at[place],
        )
        result.start()
        results.append(result)
        if place == 0:
            for q in range(4):
                sum_far(q).start()
        if place == 1:
            for q in (2, 3):
                sum_near(q, 1).start()
        if place == 2:
            for q in (0, 1):
                sum_near(q, 0).start()
            for q in (0, 1):
                sum_far(q).wait_recv()
                pass_out[q] = pass_in[q] + image[piece(right, q)]
            for q in (0, 1):
                sum_near(q, 1).start()
        if place < SPLIT - 1:
            before(STEPS - 1, chunk_at(place + 1), (STEPS - 1) % 2)
        if place == 2:
            for q in (2, 3):
                sum_far(q).wait_recv()
                pass_out[q] = pass_in[q] + image[piece(left, q)]
            for q in (2, 3):
                sum_near(q, 0).start()
    for q in range(4):
        sum_near(q, 0).wait_recv()
        sum_near(q, 1).wait_recv()
        part[q] = image[piece(col, q)] + near_in[0, q] + near_in[1, q]
    for distance in (1, 2, 3):
        sum_depth(distance).start()
    total = part[zl]
    for distance in (1, 2, 3):
        sum_depth(distance).wait_recv()
        total = total + last_in[distance - 1]
    sum_ref[...] = total

    last = (STEPS - 1) % 2
    for c in range(SPLIT):
        each_end(x_ends, lambda side, c=c: x_copy(last, c, side, None).wait_send())
        each_end(y_ends, lambda side, c=c: y_copy(last, c, side).wait_send())
    for distance in (1, 2, 3):
        gather_z(distance).wait_send()
        sum_depth(distance).wait_send()
    for q in range(4):
        gather_relay(q).wait_send()
        sum_far(q).wait_send()
        for side in range(2):
            gather_x(q, side).wait_send()
            sum_near(q, side).wait_send()
    for result in results:
        result.wait()


def shards(
    adjoint_prior,
    adjoint_now,
    forward_saved,
    residuals,
    receiver_x,
    receiver_y,
    source_x,
    source_y,
    saved_slot,
    model,
):
    _, depth, span_x, span_y = adjoint_now.shape
    layers = depth // SPLIT
    tiles = span_x // 8
    anywhere = pl.BlockSpec(memory_space=pl.ANY)
    vmem = pl.BlockSpec(memory_space=pltpu.VMEM)
    smem = pl.BlockSpec(memory_space=pltpu.SMEM)
    dma = pltpu.SemaphoreType.DMA
    state, summed = pl.pallas_call(
        kernel,
        out_shape=(
            jax.ShapeDtypeStruct(adjoint_now.shape, F32),
            jax.ShapeDtypeStruct(model.shape, F32),
        ),
        in_specs=[anywhere, anywhere, anywhere, vmem, vmem, vmem, smem, smem, smem, vmem],
        out_specs=(anywhere, vmem),
        scratch_shapes=[
            pltpu.VMEM((2, depth + 16, span_x + 16, span_y), F32),
            pltpu.VMEM((depth, span_x, span_y), F32),
            pltpu.VMEM((2, depth, span_x, span_y), F32),
            pltpu.VMEM((depth, span_x, span_y), F32),
            pltpu.VMEM((STEPS, span_x, span_y), F32),
            pltpu.VMEM((layers, span_x, span_y), F32),
            pltpu.VMEM((512, 256), BF16),
            pltpu.VMEM((2, layers * span_x, layers * span_x), BF16),
            pltpu.VMEM((2, SPLIT, 2, layers, 16, span_y), F32),
            pltpu.VMEM((2, SPLIT, tiles, 8, span_y), F32),
            pltpu.VMEM((2, SPLIT, 2, tiles, 8, span_y), F32),
            pltpu.VMEM((4, 2, span_x, span_y), F32),
            pltpu.VMEM((4, 2, span_x, span_y), F32),
            pltpu.VMEM((2, 4, 2, span_x, span_y), F32),
            pltpu.VMEM((4, 2, span_x, span_y), F32),
            pltpu.VMEM((3, 2, span_x, span_y), F32),
            dma((4,)),
            dma((2, SPLIT, 2)),
            dma((2, SPLIT, 2)),
            dma((2, SPLIT, 2)),
            dma((2, SPLIT, 2)),
            dma((3,)),
            dma((3,)),
            dma((4, 2)),
            dma((4, 2)),
            dma((4,)),
            dma((4,)),
            dma((4,)),
            dma((4,)),
            dma((4, 2)),
            dma((4, 2)),
            dma((3,)),
            dma((3,)),
        ],
        compiler_params=pltpu.CompilerParams(
            collective_id=0, has_side_effects=True, vmem_limit_bytes=63 * 1024 * 1024
        ),
    )(
        adjoint_prior,
        adjoint_now,
        forward_saved,
        jnp.swapaxes(residuals, 0, 1),
        receiver_x,
        receiver_y,
        source_x,
        source_y,
        saved_slot,
        model,
    )
    gradient = summed * (1.0 / math.sqrt(lax.axis_size("shot") * STEPS))
    return state, gradient, model - step_size * gradient


def solution(mesh):
    return jax.shard_map(
        shards,
        mesh=mesh,
        in_specs=(
            P("shot", None, "tx", "ty"),
            P("shot", None, "tx", "ty"),
            P("shot", None, None, "tx", "ty"),
            P("shot", None, None),
            P("shot", None),
            P("shot", None),
            P("shot"),
            P("shot"),
            P(),
            P("shot", "tx", "ty"),
        ),
        out_specs=(P("shot", None, "tx", "ty"), P("shot", "tx", "ty"), P("shot", "tx", "ty")),
        check_vma=False,
    )
```

```python
import math

import jax
import jax.numpy as jnp
from jax import lax
from jax.experimental import pallas as pl
from jax.experimental.pallas import tpu as pltpu
from jax.sharding import PartitionSpec as P

STEPS = 10
REACH = 8
SPLIT = 4

rec_depth = 2
src_depth = 3.0
mute_radius = 10.0
step_size = 0.01

MESH = pl.DeviceIdType.MESH
F32 = jnp.float32
BF16 = jnp.bfloat16


def coefficients():
    weights_table = []
    for offset in range(1, 9):
        weights_table.append(
            2.0
            * (-1.0) ** (offset + 1)
            * math.factorial(8) ** 2
            / (offset * offset * math.factorial(8 - offset) * math.factorial(8 + offset))
        )
    centre = -2.0 * sum(weights_table)
    return (centre, weights_table)


def halves(value):
    high = value.astype(BF16)
    low = (value - high.astype(F32)).astype(BF16)
    return high, low


def kernel(
    prior_ref,
    now_ref,
    fwd_ref,
    res_ref,
    rx_ref,
    ry_ref,
    sx_ref,
    sy_ref,
    slot_ref,
    model_ref,
    out_ref,
    sum_ref,
    field,
    speed,
    saved,
    image,
    surface,
    ylap,
    band,
    comb,
    xin,
    yout,
    yin,
    pass_in,
    pass_out,
    near_in,
    part,
    last_in,
    load_sem,
    x_send,
    x_recv,
    y_send,
    y_recv,
    gz_send,
    gz_recv,
    gx_send,
    gx_recv,
    gr_send,
    gr_recv,
    ra_send,
    ra_recv,
    rb_send,
    rb_recv,
    rd_send,
    rd_recv,
):
    centre, weights = coefficients()
    depth, span_x, span_y = speed.shape
    layers = depth // SPLIT
    tiles = span_x // 8
    shot, tx, ty = lax.axis_index("shot"), lax.axis_index("tx"), lax.axis_index("ty")
    zl, col = lax.rem(shot, 4), lax.div(shot, 4)
    right, left = lax.rem(col + 1, 4), lax.rem(col + 3, 4)
    opposite = lax.rem(col + 2, 4)
    to_right = {"shot": right * 4 + zl}
    to_left = {"shot": left * 4 + zl}
    x_ends = ((tx > 0, {"tx": tx - 1}), (tx < lax.axis_size("tx") - 1, {"tx": tx + 1}))
    y_ends = ((ty > 0, {"ty": ty - 1}), (ty < lax.axis_size("ty") - 1, {"ty": ty + 1}))

    def zl_peer(distance):
        return lax.rem(zl + distance, 4)

    loads = [
        pltpu.make_async_copy(
            now_ref.at[0], field.at[0, pl.ds(8, depth), pl.ds(8, span_x), :], load_sem.at[0]
        ),
        pltpu.make_async_copy(
            prior_ref.at[0], field.at[1, pl.ds(8, depth), pl.ds(8, span_x), :], load_sem.at[1]
        ),
        pltpu.make_async_copy(fwd_ref.at[0], saved, load_sem.at[2]),
        pltpu.make_async_copy(model_ref, speed.at[pl.ds(2 * shot, 2)], load_sem.at[3]),
    ]
    for load in loads:
        load.start()

    xin[...] = jnp.zeros_like(xin)
    yin[...] = jnp.zeros_like(yin)

    barrier = pltpu.get_barrier_semaphore()
    for present, peer in x_ends + y_ends:

        @pl.when(present)
        def _(peer=peer):
            pl.semaphore_signal(barrier, inc=1, device_id=peer, device_id_type=MESH)

    for distance in (1, 2, 3):
        pl.semaphore_signal(
            barrier, inc=1, device_id={"shot": col * 4 + zl_peer(distance)}, device_id_type=MESH
        )
    for peer in (to_right, to_left):
        pl.semaphore_signal(barrier, inc=1, device_id=peer, device_id_type=MESH)
    for par in range(2):
        field[par, pl.ds(0, 8)] = jnp.zeros((8, span_x + 16, span_y), F32)
        field[par, pl.ds(depth + 8, 8)] = jnp.zeros((8, span_x + 16, span_y), F32)
        field[par, pl.ds(8, depth), pl.ds(0, 8)] = jnp.zeros((depth, 8, span_y), F32)
        field[par, pl.ds(8, depth), pl.ds(span_x + 8, 8)] = jnp.zeros((depth, 8, span_y), F32)
    neighbours = 5
    for present, _ in x_ends + y_ends:
        neighbours = neighbours + present.astype(jnp.int32)

    def gather_z(distance):
        return pltpu.make_async_remote_copy(
            src_ref=model_ref,
            dst_ref=speed.at[pl.ds(2 * shot, 2)],
            send_sem=gz_send.at[distance - 1],
            recv_sem=gz_recv.at[distance - 1],
            device_id={"shot": col * 4 + zl_peer(distance)},
            device_id_type=MESH,
        )

    def gather_x(block, side):
        where = pl.ds(2 * (col * 4 + zl_peer(4 - block)), 2)
        return pltpu.make_async_remote_copy(
            src_ref=model_ref if block == 0 else speed.at[where],
            dst_ref=speed.at[where],
            send_sem=gx_send.at[block, side],
            recv_sem=gx_recv.at[block, side],
            device_id=to_right if side else to_left,
            device_id_type=MESH,
        )

    def gather_relay(block):
        origin = left if block < 2 else right
        where = pl.ds(2 * (origin * 4 + zl_peer(4 - block)), 2)
        return pltpu.make_async_remote_copy(
            src_ref=speed.at[where],
            dst_ref=speed.at[where],
            send_sem=gr_send.at[block],
            recv_sem=gr_recv.at[block],
            device_id=to_right if block < 2 else to_left,
            device_id_type=MESH,
        )

    def x_copy(par, c, side, source):
        zs = pl.ds(layers * c, layers)
        if source is None:
            src = field.at[par, pl.ds(8 + layers * c, layers), pl.ds(8 + (span_x - 8) * side, 8), :]
        else:
            src = source.at[0, zs, pl.ds((span_x - 8) * side, 8), :]
        return pltpu.make_async_remote_copy(
            src_ref=src,
            dst_ref=xin.at[par, c, 1 - side, :, pl.ds(8 * (1 - side), 8), :],
            send_sem=x_send.at[par, c, side],
            recv_sem=x_recv.at[par, c, 1 - side],
            device_id=x_ends[side][1],
            device_id_type=MESH,
        )

    def y_copy(par, c, side):
        return pltpu.make_async_remote_copy(
            src_ref=yout.at[par, c],
            dst_ref=yin.at[par, c, 1 - side],
            send_sem=y_send.at[par, c, side],
            recv_sem=y_recv.at[par, c, 1 - side],
            device_id=y_ends[side][1],
            device_id_type=MESH,
        )

    def each_end(ends, action):
        for side in range(2):

            @pl.when(ends[side][0])
            def _(side=side):
                action(side)

    lane = lax.broadcasted_iota(jnp.int32, (8, span_y), 1)
    group = lax.div(lane, 16)
    from_left = lax.rem(lane, 16) < 8

    def pack_y(par, c):
        for t in range(tiles):
            packed = jnp.zeros((8, span_y), F32)
            for j in range(layers):
                value = field[par, 8 + layers * c + j, pl.ds(8 + 8 * t, 8), :]
                packed = jnp.where(group == j, pltpu.roll(value, (16 * j + 8) % span_y, 1), packed)
            yout[par, c, t] = packed

    loads[0].wait()
    for c in range(SPLIT):
        pack_y(0, c)
    pl.semaphore_wait(barrier, neighbours)
    for distance in (1, 2, 3):
        gather_z(distance).start()
    for side in range(2):
        gather_x(0, side).start()
    for c in range(SPLIT):
        each_end(x_ends, lambda side, c=c: x_copy(0, c, side, now_ref).start())
    for c in range(SPLIT):
        each_end(y_ends, lambda side, c=c: y_copy(0, c, side).start())

    row = lax.broadcasted_iota(jnp.int32, (span_y, span_y), 0)
    column = lax.broadcasted_iota(jnp.int32, (span_y, span_y), 1)
    away = jnp.abs(row - column)
    inner = lax.rem(row, 16)
    halo_away = jnp.where(inner < 8, column + 8 - inner, span_y - 8 + inner - column)
    own = jnp.zeros((span_y, span_y), F32)
    edge = jnp.zeros((span_y, span_y), F32)
    for k in range(1, 9):
        own = jnp.where(away == k, F32(weights[k - 1]), own)
        edge = jnp.where(halo_away == k, F32(weights[k - 1]), edge)
    for i, matrix in enumerate((own, edge)):
        high, low = halves(matrix)
        band[pl.ds(256 * i, 128), pl.ds(0, 128)] = high
        band[pl.ds(256 * i, 128), pl.ds(128, 128)] = low
        band[pl.ds(256 * i + 128, 128), pl.ds(0, 128)] = high
        band[pl.ds(256 * i + 128, 128), pl.ds(128, 128)] = jnp.zeros((128, 128), BF16)

    cells = layers * span_x
    row = lax.broadcasted_iota(jnp.int32, (cells, cells), 0)
    column = lax.broadcasted_iota(jnp.int32, (cells, cells), 1)
    away = jnp.where(lax.div(row, span_x) == lax.div(column, span_x), jnp.abs(row - column), 0)
    inner = jnp.zeros((cells, cells), F32)
    for k in range(1, 9):
        inner = jnp.where(away == k, F32(weights[k - 1]), inner)
    comb[0], comb[1] = halves(inner)

    count = rx_ref.shape[1]
    local_x = rx_ref[...] - tx * span_x
    local_y = ry_ref[...] - ty * span_y
    at_x = local_x == lax.broadcasted_iota(jnp.int32, (span_x, count), 0)
    at_y = (local_y == lax.broadcasted_iota(jnp.int32, (span_y, count), 0)).astype(F32).astype(BF16)

    def spread(moment, carry):
        traces = jnp.where(at_x, res_ref[moment], 0.0)
        high = traces.astype(BF16)
        rest = traces - high.astype(F32)
        mid = rest.astype(BF16)
        low = (rest - mid.astype(F32)).astype(BF16)
        total = jnp.zeros((span_x, span_y), F32)
        for term in (low, mid, high):
            total = total + lax.dot_general(
                term, at_y, (((1,), (1,)), ((), ())), preferred_element_type=F32
            )
        surface[moment] = total
        return carry

    lax.fori_loop(0, STEPS, spread, 0)

    def chunk_at(place):
        return lax.rem(col + (2, 1, 3, 0)[place], SPLIT)

    def stencil(par, c, store):
        base = layers * c
        value = field[par, pl.ds(8 + base, layers), pl.ds(8, span_x), :].reshape(
            layers * span_x, span_y
        )
        high, low = halves(value)
        halo = []
        for t in range(tiles):
            halo.append(jnp.where(from_left, yin[par, c, 0, t], yin[par, c, 1, t]))
        halo = jnp.concatenate(halo, axis=0)
        groups = lax.div(lax.broadcasted_iota(jnp.int32, (span_x, span_y), 1), 16)
        halo = jnp.concatenate([jnp.where(groups == j, halo, 0.0) for j in range(layers)], axis=0)
        halo_high, halo_low = halves(halo)
        sides = jnp.dot(
            jnp.concatenate([high, low, halo_high, halo_low], axis=1),
            band[...],
            preferred_element_type=F32,
        )
        across = jnp.dot(
            comb[0], jnp.concatenate([high, low], axis=1), preferred_element_type=F32
        )
        across_low = jnp.dot(comb[1], high, preferred_element_type=F32)
        both = sides + across
        ylap[...] = (both[:, :span_y] + both[:, span_y:] + across_low).reshape(
            layers, span_x, span_y
        )
        for t in range(tiles):
            rows = pl.ds(8 + 8 * t, 8)
            plane = [field[par, base + i, rows, :] for i in range(layers + 16)]
            made = []
            for j in range(layers):
                here = plane[8 + j]
                total = F32(3.0 * centre) * here
                for k in range(1, 9):
                    pairs = plane[8 + j + k] + plane[8 + j - k]
                    total = total + F32(weights[k - 1]) * pairs
                made.append((here, total + ylap[j, pl.ds(8 * t, 8), :]))
            store(t, made)

    def add_receivers(n, c, par):
        @pl.when(c == 0)
        def _():
            at = (1 - par, 8 + rec_depth, pl.ds(8, span_x))
            field[at] = field[at] + surface[STEPS - 1 - n]

    def before(n, c, par):
        each_end(x_ends, lambda side: x_copy(1 - par, c, side, None).wait_send())
        each_end(y_ends, lambda side: y_copy(1 - par, c, side).wait_send())
        each_end(y_ends, lambda side: y_copy(par, c, 1 - side).wait_recv())
        base = layers * c

        def store(t, made):
            rows = pl.ds(8 + 8 * t, 8)
            new = [
                2.0 * here
                - field[1 - par, 8 + base + j, rows, :]
                + speed[base + j, pl.ds(8 * t, 8), :] * total
                for j, (here, total) in enumerate(made)
            ]
            for j in range(layers):
                field[1 - par, 8 + base + j, rows, :] = new[j]

        stencil(par, c, store)
        add_receivers(n, c, par)

    def before_first(c):
        each_end(y_ends, lambda side: y_copy(0, c, 1 - side).wait_recv())
        base = layers * c

        def store(t, made):
            for j in range(layers):
                image[base + j, pl.ds(8 * t, 8), :] = made[j][1]

        stencil(0, c, store)

    def finish_first(c):
        zs = pl.ds(layers * c, layers)
        inside = (pl.ds(8 + layers * c, layers), pl.ds(8, span_x))
        field[(1,) + inside] = (
            2.0 * field[(0,) + inside] - field[(1,) + inside] + speed[zs] * image[zs]
        )
        add_receivers(0, c, 0)

    def after(c, par, onward=True):
        base = layers * c

        def outer_tile(side):
            rows = pl.ds(8 + (span_x - 8) * side, 8)
            new = []
            for j in range(layers):
                total = jnp.zeros((8, span_y), F32)
                for k in range(1, 9):
                    start = k if side else 8 - k
                    total = total + F32(weights[k - 1]) * xin[par, c, side, j, pl.ds(start, 8), :]
                new.append(
                    field[1 - par, 8 + base + j, rows, :]
                    + speed[base + j, pl.ds((span_x - 8) * side, 8), :] * total
                )
            for j in range(layers):
                field[1 - par, 8 + base + j, rows, :] = new[j]

        for parity in range(2):

            @pl.when(lax.rem(tx, 2) == parity)
            def _(parity=parity):
                for side in (parity, 1 - parity):

                    @pl.when(x_ends[side][0])
                    def _(side=side):
                        x_copy(par, c, 1 - side, None).wait_recv()
                        outer_tile(side)
                        if onward:
                            x_copy(1 - par, c, side, None).start()

    def send(c, nxt):
        pack_y(nxt, c)
        each_end(y_ends, lambda side: y_copy(nxt, c, side).start())

    def imaged(n, c, nxt):
        zs = pl.ds(layers * c, layers)
        inside = (nxt, pl.ds(8 + layers * c, layers), pl.ds(8, span_x))
        return saved[slot_ref[STEPS - 1 - n], zs] * field[inside]

    for block in (1, 2, 3):
        gather_z(block).wait_recv()
        for side in range(2):
            gather_x(block, side).start()
    for place in (0, 1):
        before_first(chunk_at(place))
    for block in range(4):
        gather_x(block, 1).wait_recv()
        if block < 2:
            gather_relay(block).start()
        gather_x(block, 0).wait_recv()
        if block >= 2:
            gather_relay(block).start()
    for place in (2, 3):
        before_first(chunk_at(place))
    loads[1].wait()
    for block in range(4):
        gather_relay(block).wait_recv()
    loads[3].wait()

    for place in range(SPLIT):
        c = chunk_at(place)
        finish_first(c)
        after(c, 0)
        send(c, 1)
        if place == 0:
            loads[2].wait()
        image[pl.ds(layers * c, layers)] = imaged(0, c, 1)
    before(1, chunk_at(0), 1)

    def two_steps(pair, carry):
        for half in range(2):
            n = 1 + 2 * pair + half
            par = 1 - half
            for place in range(SPLIT):
                c = chunk_at(place)
                after(c, par)
                send(c, 1 - par)
                zs = pl.ds(layers * c, layers)
                image[zs] = image[zs] + imaged(n, c, 1 - par)
                if place < SPLIT - 1:
                    before(n, chunk_at(place + 1), par)
                else:
                    before(n + 1, chunk_at(0), 1 - par)
        return carry

    lax.fori_loop(0, (STEPS - 2) // 2, two_steps, 0)

    sx = sx_ref[0].astype(F32)
    sy = sy_ref[0].astype(F32)
    cell_x = (tx * span_x + lax.broadcasted_iota(jnp.int32, (span_x, span_y), 0)).astype(F32) - sx
    cell_y = (ty * span_y + lax.broadcasted_iota(jnp.int32, (span_x, span_y), 1)).astype(F32) - sy
    flat = cell_x * cell_x + cell_y * cell_y

    def piece(column_at, q):
        return pl.ds(8 * column_at + 2 * q, 2)

    def sum_far(q):
        return pltpu.make_async_remote_copy(
            src_ref=image.at[piece(opposite, q)],
            dst_ref=pass_in.at[q],
            send_sem=ra_send.at[q],
            recv_sem=ra_recv.at[q],
            device_id=to_right if q < 2 else to_left,
            device_id_type=MESH,
        )

    def sum_near(q, side):
        combined = (q < 2) == (side == 1)
        return pltpu.make_async_remote_copy(
            src_ref=pass_out.at[q] if combined else image.at[piece(right if side else left, q)],
            dst_ref=near_in.at[1 - side, q],
            send_sem=rb_send.at[q, side],
            recv_sem=rb_recv.at[q, 1 - side],
            device_id=to_right if side else to_left,
            device_id_type=MESH,
        )

    def sum_depth(distance):
        return pltpu.make_async_remote_copy(
            src_ref=part.at[zl_peer(distance)],
            dst_ref=last_in.at[distance - 1],
            send_sem=rd_send.at[distance - 1],
            recv_sem=rd_recv.at[distance - 1],
            device_id={"shot": col * 4 + zl_peer(distance)},
            device_id_type=MESH,
        )

    results = []
    for place in range(SPLIT):
        c = chunk_at(place)
        after(c, (STEPS - 1) % 2, onward=False)
        zs = pl.ds(layers * c, layers)
        muted = image[zs] + imaged(STEPS - 1, c, STEPS % 2)
        for j in range(layers):
            gap = (layers * c + j).astype(F32) - src_depth
            image[layers * c + j] = muted[j] * (
                1.0 - jnp.exp(-(gap * gap + flat) / (mute_radius * mute_radius))
            )
        result = pltpu.make_async_copy(
            field.at[STEPS % 2, pl.ds(8 + layers * c, layers), pl.ds(8, span_x), :],
            out_ref.at[0, zs],
            load_sem.at[place],
        )
        result.start()
        results.append(result)
        if place == 0:
            for q in range(4):
                sum_far(q).start()
        if place == 1:
            for q in (2, 3):
                sum_near(q, 1).start()
        if place == 2:
            for q in (0, 1):
                sum_near(q, 0).start()
            for q in (0, 1):
                sum_far(q).wait_recv()
                pass_out[q] = pass_in[q] + image[piece(right, q)]
            for q in (0, 1):
                sum_near(q, 1).start()
        if place < SPLIT - 1:
            before(STEPS - 1, chunk_at(place + 1), (STEPS - 1) % 2)
        if place == 2:
            for q in (2, 3):
                sum_far(q).wait_recv()
                pass_out[q] = pass_in[q] + image[piece(left, q)]
            for q in (2, 3):
                sum_near(q, 0).start()
    for q in range(4):
        sum_near(q, 0).wait_recv()
        sum_near(q, 1).wait_recv()
        part[q] = image[piece(col, q)] + near_in[0, q] + near_in[1, q]
    for distance in (1, 2, 3):
        sum_depth(distance).start()
    total = part[zl]
    for distance in (1, 2, 3):
        sum_depth(distance).wait_recv()
        total = total + last_in[distance - 1]
    sum_ref[...] = total

    last = (STEPS - 1) % 2
    for c in range(SPLIT):
        each_end(x_ends, lambda side, c=c: x_copy(last, c, side, None).wait_send())
        each_end(y_ends, lambda side, c=c: y_copy(last, c, side).wait_send())
    for distance in (1, 2, 3):
        gather_z(distance).wait_send()
        sum_depth(distance).wait_send()
    for q in range(4):
        gather_relay(q).wait_send()
        sum_far(q).wait_send()
        for side in range(2):
            gather_x(q, side).wait_send()
            sum_near(q, side).wait_send()
    for result in results:
        result.wait()


def shards(
    adjoint_prior,
    adjoint_now,
    forward_saved,
    residuals,
    receiver_x,
    receiver_y,
    source_x,
    source_y,
    saved_slot,
    model,
):
    _, depth, span_x, span_y = adjoint_now.shape
    layers = depth // SPLIT
    tiles = span_x // 8
    anywhere = pl.BlockSpec(memory_space=pl.ANY)
    vmem = pl.BlockSpec(memory_space=pltpu.VMEM)
    smem = pl.BlockSpec(memory_space=pltpu.SMEM)
    dma = pltpu.SemaphoreType.DMA
    state, summed = pl.pallas_call(
        kernel,
        out_shape=(
            jax.ShapeDtypeStruct(adjoint_now.shape, F32),
            jax.ShapeDtypeStruct(model.shape, F32),
        ),
        in_specs=[anywhere, anywhere, anywhere, vmem, vmem, vmem, smem, smem, smem, vmem],
        out_specs=(anywhere, vmem),
        scratch_shapes=[
            pltpu.VMEM((2, depth + 16, span_x + 16, span_y), F32),
            pltpu.VMEM((depth, span_x, span_y), F32),
            pltpu.VMEM((2, depth, span_x, span_y), F32),
            pltpu.VMEM((depth, span_x, span_y), F32),
            pltpu.VMEM((STEPS, span_x, span_y), F32),
            pltpu.VMEM((layers, span_x, span_y), F32),
            pltpu.VMEM((512, 256), BF16),
            pltpu.VMEM((2, layers * span_x, layers * span_x), BF16),
            pltpu.VMEM((2, SPLIT, 2, layers, 16, span_y), F32),
            pltpu.VMEM((2, SPLIT, tiles, 8, span_y), F32),
            pltpu.VMEM((2, SPLIT, 2, tiles, 8, span_y), F32),
            pltpu.VMEM((4, 2, span_x, span_y), F32),
            pltpu.VMEM((4, 2, span_x, span_y), F32),
            pltpu.VMEM((2, 4, 2, span_x, span_y), F32),
            pltpu.VMEM((4, 2, span_x, span_y), F32),
            pltpu.VMEM((3, 2, span_x, span_y), F32),
            dma((4,)),
            dma((2, SPLIT, 2)),
            dma((2, SPLIT, 2)),
            dma((2, SPLIT, 2)),
            dma((2, SPLIT, 2)),
            dma((3,)),
            dma((3,)),
            dma((4, 2)),
            dma((4, 2)),
            dma((4,)),
            dma((4,)),
            dma((4,)),
            dma((4,)),
            dma((4, 2)),
            dma((4, 2)),
            dma((3,)),
            dma((3,)),
        ],
        compiler_params=pltpu.CompilerParams(
            collective_id=0, has_side_effects=True, vmem_limit_bytes=63 * 1024 * 1024
        ),
    )(
        adjoint_prior,
        adjoint_now,
        forward_saved,
        jnp.swapaxes(residuals, 0, 1),
        receiver_x,
        receiver_y,
        source_x,
        source_y,
        saved_slot,
        model,
    )
    gradient = summed * (1.0 / math.sqrt(lax.axis_size("shot") * STEPS))
    return state, gradient, model - step_size * gradient


def solution(mesh):
    return jax.shard_map(
        shards,
        mesh=mesh,
        in_specs=(
            P("shot", None, "tx", "ty"),
            P("shot", None, "tx", "ty"),
            P("shot", None, None, "tx", "ty"),
            P("shot", None, None),
            P("shot", None),
            P("shot", None),
            P("shot"),
            P("shot"),
            P(),
            P("shot", "tx", "ty"),
        ),
        out_specs=(P("shot", None, "tx", "ty"), P("shot", "tx", "ty"), P("shot", "tx", "ty")),
        check_vma=False,
    )
```
